256 devices in a mesh: leaf: 8 (over y, core), front: 32 (over x, z).
Axes of the slice: x: 4, y: 4, z: 8, core: 2. Of those that a mesh axis runs over, the one named last changes fastest.
Arguments:
- child_fronts: float32 [8, 4096, 1, 32, 128], P('leaf', None, None, 'front'), as said below
- parent_front: float32 [8, 8, 128, 2, 32, 128], P(None, 'leaf', None, None, 'front'), as said below
- child_map: int32 [8, 24], replicated, may hold values from 0 to 63, as said below
Outputs:
- child_result: float32 [8, 4096, 1, 32, 128], P('leaf', None, None, 'front')
- parent_result: float32 [8, 8, 128, 2, 32, 128], P(None, 'leaf', None, None, 'front')
The draws below stay inside these ranges and needn't reach their ends.
Inputs may be any that keep to these rules, and one draw needn't show every extreme that they name: Row g gives, for each update block v of child g, the parent block that receives it. The entries of a row are distinct, child_map[g, v] mod 32 equals (8 + v) mod 32, and every child's last update block goes to the parent's last block. `child_fronts`: each front is symmetric positive definite. `parent_front`: the parent front is symmetric positive definite.
All inputs are finite; a program needn't handle non-finite values.
Results may differ from the reference program's by a relative error of at most 0.000059.
Values sent between devices are 32-bit elements; how exact they have to be, the bound alone decides.
No kernel may reach another device: no remote copies, remote signals or barrier semaphores. Data moves between devices by JAX's collectives and lax.ppermute only.
A program may use at most 256 MiB of HBM per device.

```python
import jax
import jax.numpy as jnp
from jax import lax

BLK = 128
CHILD_ORDER = 4096
CHILD_PIVOTS = 8
PARENT_ORDER = 8192
PARENT_PIVOTS = 2
GROUPS = 8
UPDATE_BLOCKS = 24
CHILD_SLOTS = 1
PARENT_RSLOTS = 8
PARENT_CSLOTS = 2


def symmetric_front(key, order):
    key_raw = jax.random.fold_in(key, 0)
    raw = jax.random.normal(key_raw, (order, order), jnp.float32)
    gram = jnp.dot(raw, raw.T, precision=lax.Precision.HIGHEST) * (1.0 / order)
    gram = 0.5 * (gram + gram.T)
    positions = jnp.arange(order, dtype=jnp.int32)
    shifted = gram + jnp.where(positions[:, None] == positions[None, :], 0.15, 0.0).astype(jnp.float32)
    return shifted


def draw_child_fronts(key, part):
    keys = jax.random.split(jax.random.fold_in(key, 11), GROUPS)
    fronts = lax.map(lambda single: symmetric_front(single, CHILD_ORDER), keys)
    return fronts.reshape(GROUPS, CHILD_ORDER, CHILD_SLOTS, -1, BLK)


def draw_parent_front(key, part):
    matrix = symmetric_front(jax.random.fold_in(key, 23), PARENT_ORDER)
    leaf_count = PARENT_ORDER // BLK // PARENT_RSLOTS
    front_count = PARENT_ORDER // BLK // PARENT_CSLOTS
    return matrix.reshape(PARENT_RSLOTS, leaf_count, BLK, PARENT_CSLOTS, front_count, BLK)


def draw_child_map(key, part):
    front_count = PARENT_ORDER // BLK // PARENT_CSLOTS
    positions = CHILD_PIVOTS + jnp.arange(UPDATE_BLOCKS, dtype=jnp.int32)
    residues = positions % front_count
    ranks = positions // front_count
    last_rank = (CHILD_PIVOTS + UPDATE_BLOCKS - 1) // front_count
    scores = jax.random.randint(jax.random.fold_in(key, 37), (GROUPS, front_count, PARENT_CSLOTS), 0, 1 << 20)
    scores = scores * PARENT_CSLOTS + jnp.arange(PARENT_CSLOTS, dtype=jnp.int32)[None, None, :]
    top_slot = (jnp.arange(front_count, dtype=jnp.int32)[:, None] == front_count - 1) & (jnp.arange(PARENT_CSLOTS, dtype=jnp.int32)[None, :] == PARENT_CSLOTS - 1)
    scores = jnp.where(top_slot[None, :, :], -1, scores)
    orders = jnp.argsort(scores, axis=-1, stable=True).astype(jnp.int32)
    picks = (ranks - last_rank) % PARENT_CSLOTS
    chosen = orders[:, residues, picks]
    return (residues[None, :] + front_count * chosen).astype(jnp.int32)


def setup_inputs(seed: int = 0) -> dict:
    arg_keys = jax.random.split(jax.random.key(seed), 4)
    return {
        "child_fronts": draw_child_fronts(jax.random.fold_in(arg_keys[3], 71), 0),
        "parent_front": draw_parent_front(jax.random.fold_in(arg_keys[3], 71), 0),
        "child_map": draw_child_map(jax.random.fold_in(arg_keys[3], 71), 0),
    }


def partial_factor(front, pivots):
    order = front.shape[0]
    factor = jnp.linalg.cholesky(front[:pivots, :pivots])
    lower_part = jax.scipy.linalg.solve_triangular(factor, front[pivots:, :pivots].T, lower=True).T
    schur = front[pivots:, pivots:] - jnp.dot(lower_part, lower_part.T, precision=lax.Precision.HIGHEST)
    upper = jnp.concatenate([factor, jnp.zeros((pivots, order - pivots), front.dtype)], 1)
    bottom = jnp.concatenate([lower_part, schur], 1)
    return jnp.concatenate([upper, bottom], 0)

def reference(child_fronts, parent_front, child_map):
    groups = child_fronts.shape[0]
    fronts = child_fronts.reshape(groups, CHILD_ORDER, CHILD_ORDER)
    pivot_rows = CHILD_PIVOTS * BLK
    results = lax.map(lambda single: partial_factor(single, pivot_rows), fronts)
    parent = parent_front.reshape(PARENT_ORDER, PARENT_ORDER)
    offsets = jnp.arange(BLK, dtype=jnp.int32)
    for group in range(groups):
        targets = (child_map[group].astype(jnp.int32)[:, None] * BLK + offsets[None, :]).reshape(-1)
        parent = parent.at[targets[:, None], targets[None, :]].add(results[group, pivot_rows:, pivot_rows:])
    parent = partial_factor(parent, PARENT_PIVOTS * BLK)
    return (results.reshape(child_fronts.shape), parent.reshape(parent_front.shape))
```

```python
import jax, jax.numpy as jnp
from jax import lax
from jax.experimental import pallas as pl
from jax.experimental.pallas import tpu as pltpu
from jax.sharding import PartitionSpec as P

BLK=128
CHILD_PIVOTS=8
PARENT_PIVOTS=2
PARENT_CSLOTS=2
NB=16
HI=lax.Precision.HIGHEST

def mm(a,b):
    return jnp.dot(a,b,precision=HI,preferred_element_type=jnp.float32)

def factor_block(a, u_ref, m_ref, nb=None):
    nb = nb or NB
    n=BLK
    rows=lax.broadcasted_iota(jnp.int32,(n,n),0); cols=lax.broadcasted_iota(jnp.int32,(n,n),1)
    inv=jnp.where(rows==cols,1.0,0.0).astype(jnp.float32)
    sub=lax.broadcasted_iota(jnp.int32,(nb,n),0)
    lane=lax.broadcasted_iota(jnp.int32,(nb,n),1)
    for c0 in range(0,n,nb):
        r=a[c0:c0+nb,:]; y=inv[c0:c0+nb,:]
        bc=[jnp.broadcast_to(r[:,c0+t:c0+t+1],(nb,n)) for t in range(nb)]
        piv=jnp.ones((nb,n),jnp.float32)
        for t in range(nb):
            p=jnp.broadcast_to(bc[t][t:t+1,:],(nb,n))
            piv=jnp.where(sub==t,p,piv)
            if t==nb-1: break
            m=jnp.where(sub>t,bc[t]*(1.0/p),0.0)
            for q in range(t+1,nb):
                bc[q]=bc[q]-m*jnp.broadcast_to(bc[q][t:t+1,:],(nb,n))
            r=r-m*jnp.broadcast_to(r[t:t+1,:],(nb,n))
            y=y-m*jnp.broadcast_to(y[t:t+1,:],(nb,n))
        scale=lax.rsqrt(piv)
        u=jnp.where(lane>=sub+c0,r*scale,0.0); y=y*scale
        u_ref[c0:c0+nb,:]=u; m_ref[c0:c0+nb,:]=y
        if c0+nb<n:
            upd=mm(u.T,jnp.concatenate([u,y],1))
            a=a-upd[:,:n]; inv=inv-upd[:,n:]

def child_kernel(pos_ref, ring_ref, own_ref, z_ref, col_ref, a_ref, y_ref, v_ref, u_ref, m_ref):
    front=pos_ref[0]; zpos=pos_ref[1]; nblk=8; n=BLK*nblk
    for k in range(nblk):
        a_ref[:, k*BLK:(k+1)*BLK]=ring_ref[(k-zpos+nblk)%nblk]
    y_ref[...]=jnp.zeros((n,n),jnp.float32)
    v_ref[...]=own_ref[...]
    z_ref[...]=jnp.zeros((n,BLK),jnp.float32)
    col_ref[...]=jnp.zeros((n,BLK),jnp.float32)
    rows=lax.broadcasted_iota(jnp.int32,(BLK,BLK),0); cols=lax.broadcasted_iota(jnp.int32,(BLK,BLK),1)
    eye=jnp.where(rows==cols,1.0,0.0).astype(jnp.float32)
    def step(k,carry):
        for s in range(nblk):
            @pl.when(k==s)
            def _(s=s):
                m_ref[...]=a_ref[s*BLK:(s+1)*BLK,s*BLK:(s+1)*BLK]
        factor_block(m_ref[...],u_ref,m_ref)
        for s in range(nblk):
            @pl.when(k==s)
            def _(s=s):
                lo=s*BLK; hi=lo+BLK
                m=m_ref[...]
                parts=[]
                if s: parts.append(y_ref[lo:hi,:lo])
                if hi<n: parts.append(a_ref[lo:hi,hi:])
                parts.append(v_ref[lo:hi,:])
                full=mm(m,jnp.concatenate(parts,1))
                yk=jnp.concatenate([full[:,:lo],m],1) if s else m
                rest=full[:,lo:n-BLK]; vk=full[:,n-BLK:]
                if hi<n:
                    upd=mm(rest.T,jnp.concatenate([yk,rest,vk],1))
                    y_ref[hi:,:hi]-=upd[:,:hi]
                    a_ref[hi:,hi:]-=upd[:,hi:n]
                    v_ref[hi:,:]-=upd[:,n:]
                vk=jnp.where(front<nblk,jnp.where(front==s,eye,0.0),vk)
                z_ref[:hi,:]+=mm(yk.T,vk)
                @pl.when(front==s)
                def _():
                    col_ref[lo:hi,:]=u_ref[...].T
                    for j in range(s+1,nblk):
                        col_ref[j*BLK:(j+1)*BLK,:]=rest[:,(j-s-1)*BLK:(j-s)*BLK].T
        return carry
    lax.fori_loop(0,nblk,step,0)

def child_factor(pos,ring,own):
    n=own.shape[0]
    return pl.pallas_call(child_kernel,
        out_shape=(jax.ShapeDtypeStruct((n,BLK),jnp.float32),)*2,
        in_specs=[pl.BlockSpec(memory_space=pltpu.SMEM),pl.BlockSpec(memory_space=pltpu.VMEM),pl.BlockSpec(memory_space=pltpu.VMEM)],
        out_specs=(pl.BlockSpec(memory_space=pltpu.VMEM),)*2,
        scratch_shapes=[pltpu.VMEM((n,n),jnp.float32),pltpu.VMEM((n,n),jnp.float32),pltpu.VMEM((n,BLK),jnp.float32),pltpu.VMEM((BLK,BLK),jnp.float32),pltpu.VMEM((BLK,BLK),jnp.float32)],
        compiler_params=pltpu.CompilerParams(vmem_limit_bytes=40<<20),
        name="child_factor")(pos,ring,own)


def split(a):
    hi=a.astype(jnp.bfloat16)
    return hi,(a-hi.astype(jnp.float32)).astype(jnp.bfloat16)

def mm3(a,b):
    ah,al=split(a); bh,bl=split(b)
    dot=lambda x,y: jnp.dot(x,y,preferred_element_type=jnp.float32)
    return dot(ah,bh)+(dot(ah,bl)+dot(al,bh))

UPD=4

def update_kernel(pos_ref, g_ref, z_ref, col_ref, own_ref, out_ref, zh_ref, zl_ref):
    front=pos_ref[0]; step=pl.program_id(0); head=col_ref.shape[0]//(UPD*BLK)
    @pl.when(step==0)
    def _():
        zh,zl=split(z_ref[...].T)
        zh_ref[...]=zh; zl_ref[...]=zl
    @pl.when(step<head)
    def _():
        out_ref[...]=col_ref[pl.ds(pl.multiple_of(step*UPD*BLK,UPD*BLK),UPD*BLK),:]
    @pl.when(step>=head)
    def _():
        dot=lambda x,y: jnp.dot(x,y,preferred_element_type=jnp.float32)
        sign=jnp.where(front<CHILD_PIVOTS,-1.0,1.0).astype(jnp.float32)
        for b in range(UPD):
            gh,gl=split(g_ref[b])
            zh=zh_ref[...]
            prod=dot(zh,gh)+(dot(zh,gl)+dot(zl_ref[...],gh))
            base=own_ref[b*BLK:(b+1)*BLK,:]
            out_ref[b*BLK:(b+1)*BLK,:]=jnp.where(front<CHILD_PIVOTS,0.0,base)-sign*prod.T

def child_update(pos,gathered,z,col,own):
    rows=own.shape[0]; piv=col.shape[0]; head=piv//(UPD*BLK)
    return pl.pallas_call(update_kernel,
        out_shape=jax.ShapeDtypeStruct((rows,BLK),jnp.float32),
        grid=(rows//(UPD*BLK),),
        in_specs=[pl.BlockSpec(memory_space=pltpu.SMEM),
            pl.BlockSpec((UPD,piv,BLK),lambda i:(jnp.maximum(i,head),0,0)),
            pl.BlockSpec((piv,BLK),lambda i:(0,0)),
            pl.BlockSpec((piv,BLK),lambda i:(0,0)),
            pl.BlockSpec((UPD*BLK,BLK),lambda i:(i,0))],
        out_specs=pl.BlockSpec((UPD*BLK,BLK),lambda i:(i,0)),
        scratch_shapes=[pltpu.VMEM((BLK,piv),jnp.bfloat16),pltpu.VMEM((BLK,piv),jnp.bfloat16)],
        compiler_params=pltpu.CompilerParams(vmem_limit_bytes=40<<20),
        name="child_update")(pos,gathered,z,col,own)

def parent_kernel(pos_ref, p11_ref, wc_ref, wr_ref, par_ref, out_ref, u_ref, m_ref):
    front=pos_ref[0]; leaf=pos_ref[1]
    slots=wr_ref.shape[0]; cs=wc_ref.shape[0]
    a0=p11_ref[0]; a1=p11_ref[1]
    factor_block(a0[:BLK],u_ref,m_ref)
    m0=m_ref[...]; u00=u_ref[...]
    u01=mm(m0,a1[:BLK])
    u_ref[...]=a1[BLK:]-mm(u01.T,u01)
    factor_block(u_ref[...],u_ref,m_ref)
    m1=m_ref[...]; u11=u_ref[...]
    w=jnp.concatenate([wc_ref[c] for c in range(cs)]+[wr_ref[s] for s in range(slots)],1)
    v0=mm(m0,w[:BLK])
    v1=mm(m1,w[BLK:]-mm(u01.T,v0))
    v=jnp.concatenate([v0,v1],0)
    lrows=v[:,cs*BLK:].T
    prod=mm(lrows,v[:,:cs*BLK])
    for s in range(slots):
        for c in range(cs):
            at=pl.ds(s*BLK*cs+c,BLK,stride=cs)
            out_ref[at,:]=par_ref[at,:]-prod[s*BLK:(s+1)*BLK,c*BLK:(c+1)*BLK]
    for p in range(PARENT_PIVOTS):
        @pl.when(front==p)
        def _(p=p):
            for s in range(slots):
                out_ref[pl.ds(s*BLK*cs,BLK,stride=cs),:]=lrows[s*BLK:(s+1)*BLK,p*BLK:(p+1)*BLK]
    top0=pl.ds(0,BLK,stride=cs)
    zero=jnp.zeros((BLK,BLK),jnp.float32)
    @pl.when(leaf<PARENT_PIVOTS)
    def _():
        for c in range(1,cs):
            out_ref[pl.ds(c,BLK,stride=cs),:]=zero
        @pl.when(front>=PARENT_PIVOTS)
        def _():
            out_ref[top0,:]=zero
        @pl.when((front==0)&(leaf==0))
        def _():
            out_ref[top0,:]=u00.T
        @pl.when((front==1)&(leaf==1))
        def _():
            out_ref[top0,:]=u11.T
        @pl.when((front==1)&(leaf==0))
        def _():
            out_ref[top0,:]=zero

def parent_base(pos,p11,wc,wr,par):
    vm=pl.BlockSpec(memory_space=pltpu.VMEM)
    return pl.pallas_call(parent_kernel,
        out_shape=jax.ShapeDtypeStruct(par.shape,jnp.float32),
        in_specs=[pl.BlockSpec(memory_space=pltpu.SMEM),vm,vm,vm,vm],
        out_specs=vm,
        scratch_shapes=[pltpu.VMEM((BLK,BLK),jnp.float32),pltpu.VMEM((BLK,BLK),jnp.float32)],
        compiler_params=pltpu.CompilerParams(vmem_limit_bytes=40<<20),
        name="parent_base")(pos,p11,wc,wr,par)

def extend_kernel(idx_ref, flag_ref, base_ref, recv_ref, out_ref):
    out_ref[...]=base_ref[...]
    quota,groups=recv_ref.shape[0],recv_ref.shape[1]
    cs=PARENT_CSLOTS
    @pl.when(flag_ref[0]>0)
    def _():
        for q in range(quota):
            for g in range(groups):
                start=idx_ref[q,g]
                at=pl.ds(start,BLK,stride=cs)
                out_ref[at,:]+=recv_ref[q,g]

def extend_add(idx,flag,base,recv):
    vm=pl.BlockSpec(memory_space=pltpu.VMEM); sm=pl.BlockSpec(memory_space=pltpu.SMEM)
    return pl.pallas_call(extend_kernel,
        out_shape=jax.ShapeDtypeStruct(base.shape,jnp.float32),
        in_specs=[sm,sm,vm,vm], out_specs=vm,
        input_output_aliases={2:0},
        compiler_params=pltpu.CompilerParams(vmem_limit_bytes=40<<20),
        name="extend_add")(idx,flag,base,recv)

def body(child_fronts, parent_front, child_map):
    XS,ZS=4,8
    leaf=lax.axis_index("leaf"); front=lax.axis_index("front")
    xpos=front//ZS; zpos=front%ZS
    own=child_fronts.reshape(child_fronts.shape[1],BLK)
    piv=CHILD_PIVOTS*BLK
    top=own[:piv]
    def fperm(pairs,v):
        return lax.ppermute(v,"front",pairs)
    mine=top
    for d in range(1,XS):
        got=fperm([(z,d*ZS+z) for z in range(ZS)],top)
        mine=jnp.where(xpos==d,got,mine)
    rot=lambda d:[(x*ZS+z,x*ZS+(z+d)%ZS) for x in range(XS) for z in range(ZS)]
    ring=[None]*ZS
    ring[0]=mine; fwd=bwd=mine
    for d in range(1,ZS//2):
        fwd=fperm(rot(1),fwd); ring[(-d)%ZS]=fwd
        bwd=fperm(rot(-1),bwd); ring[d]=bwd
    half=piv//2
    ring[ZS//2]=jnp.concatenate([fperm(rot(1),fwd[:half]),fperm(rot(-1),bwd[half:])],0)
    gathered=lax.all_gather(top,"front",axis=0)
    prow=parent_front.reshape(parent_front.shape[0],BLK*PARENT_CSLOTS,BLK)
    leaves=lax.axis_size("leaf")
    def leaf_bcast(v):
        return lax.all_to_all(jnp.broadcast_to(v[None],(leaves,)+v.shape),"leaf",split_axis=0,concat_axis=0,tiled=True)
    wc=leaf_bcast(prow[0])[:PARENT_PIVOTS]
    wc=wc.reshape(PARENT_PIVOTS*BLK,PARENT_CSLOTS,BLK).transpose(1,0,2)
    both=("leaf","front")
    rel=(zpos-leaf)%ZS
    w=wc
    for s in (1,2,4):
        pairs=[(l*32+x*ZS+(l+r)%ZS, l*32+x*ZS+(l+r+s)%ZS) for l in range(ZS) for x in range(XS) for r in range(s)]
        got=lax.ppermute(w,both,pairs)
        w=jnp.where((rel>=s)&(rel<2*s),got,w)
    planes=[w]
    for d in range(1,XS):
        planes.append(fperm([(x*ZS+z,((x-d)%XS)*ZS+z) for x in range(XS) for z in range(ZS)],w))
    stack=jnp.stack(planes,0)
    stack=jnp.concatenate([stack,stack],0)
    wr=lax.dynamic_slice_in_dim(stack,(XS-xpos)%XS,XS,0)
    wr=wr.transpose(1,0,2,3).reshape(XS*PARENT_CSLOTS,PARENT_PIVOTS*BLK,BLK)
    p11=leaf_bcast(wr[0])[:PARENT_PIVOTS]
    pos=jnp.stack([front,zpos]).astype(jnp.int32)
    z,col=child_factor(pos,jnp.stack(ring,0),top)
    out=child_update(pos,gathered,z,col,own)
    quota=(own.shape[0]-piv)//BLK//leaves
    sent=out[piv:].reshape(quota,leaves,BLK,BLK)
    recv=lax.all_to_all(sent,"leaf",split_axis=1,concat_axis=1,tiled=True)
    base=parent_base(jnp.stack([front,leaf]).astype(jnp.int32),p11,wc,wr,prow.reshape(-1,BLK))
    rowsel=(jnp.arange(leaves)==leaf)
    rmap=jnp.sum(jnp.where(rowsel[None,None,:],child_map.reshape(leaves,quota,leaves),0),axis=2)
    vblk=front-CHILD_PIVOTS
    csel=(jnp.arange(child_map.shape[1])==vblk)
    cmap=jnp.sum(jnp.where(csel[None,:],child_map,0),axis=1)
    idx=((rmap//leaves)*(BLK*PARENT_CSLOTS)+(cmap//32)[:,None]).T.astype(jnp.int32)
    flag=(front>=CHILD_PIVOTS).astype(jnp.int32).reshape(1)
    parent=extend_add(idx,flag,base,recv)
    return out.reshape(child_fronts.shape),parent.reshape(parent_front.shape)


def solution(mesh):
    return jax.shard_map(
        body,
        mesh=mesh,
        in_specs=(
            P("leaf", None, None, "front", None),
            P(None, "leaf", None, None, "front", None),
            P(),
        ),
        out_specs=(
            P("leaf", None, None, "front", None),
            P(None, "leaf", None, None, "front", None),
        ),
        check_vma=False,
    )
```

```python
import jax, jax.numpy as jnp
from jax import lax
from jax.experimental import pallas as pl
from jax.experimental.pallas import tpu as pltpu
from jax.sharding import PartitionSpec as P

BLK=128
CHILD_PIVOTS=8
PARENT_PIVOTS=2
PARENT_CSLOTS=2
NB=16
HI=lax.Precision.HIGHEST

def mm(a,b):
    return jnp.dot(a,b,precision=HI,preferred_element_type=jnp.float32)

def factor_block(a, u_ref, m_ref, nb=None):
    nb = nb or NB
    n=BLK
    rows=lax.broadcasted_iota(jnp.int32,(n,n),0); cols=lax.broadcasted_iota(jnp.int32,(n,n),1)
    inv=jnp.where(rows==cols,1.0,0.0).astype(jnp.float32)
    sub=lax.broadcasted_iota(jnp.int32,(nb,n),0)
    lane=lax.broadcasted_iota(jnp.int32,(nb,n),1)
    for c0 in range(0,n,nb):
        r=a[c0:c0+nb,:]; y=inv[c0:c0+nb,:]
        bc=[jnp.broadcast_to(r[:,c0+t:c0+t+1],(nb,n)) for t in range(nb)]
        piv=jnp.ones((nb,n),jnp.float32)
        for t in range(nb):
            p=jnp.broadcast_to(bc[t][t:t+1,:],(nb,n))
            piv=jnp.where(sub==t,p,piv)
            if t==nb-1: break
            m=jnp.where(sub>t,bc[t]*(1.0/p),0.0)
            for q in range(t+1,nb):
                bc[q]=bc[q]-m*jnp.broadcast_to(bc[q][t:t+1,:],(nb,n))
            r=r-m*jnp.broadcast_to(r[t:t+1,:],(nb,n))
            y=y-m*jnp.broadcast_to(y[t:t+1,:],(nb,n))
        scale=lax.rsqrt(piv)
        u=jnp.where(lane>=sub+c0,r*scale,0.0); y=y*scale
        u_ref[c0:c0+nb,:]=u; m_ref[c0:c0+nb,:]=y
        if c0+nb<n:
            upd=mm(u.T,jnp.concatenate([u,y],1))
            a=a-upd[:,:n]; inv=inv-upd[:,n:]

def child_kernel(pos_ref, *refs):
    rhs_ref, zt_ref, col_ref, ring_ref, a_ref, y_ref, v_ref, u_ref, m_ref = refs[-9:]
    front=pos_ref[0]; zpos=pos_ref[1]; nblk=ring_ref.shape[0]; n=BLK*nblk
    planes=rhs_ref.shape[0]; half=nblk//2
    for d in range(nblk):
        if d!=half: ring_ref[d]=refs[d][...]
    hrows=ring_ref.shape[1]//2
    ring_ref[half,:hrows]=refs[half][...]
    ring_ref[half,hrows:]=refs[nblk][...]
    for k in range(nblk):
        d=(k-zpos+nblk)%nblk
        for i in range(half+1):
            r=(k+i)%nblk
            if r>k:
                if i<half: a_ref[k*BLK:(k+1)*BLK,r*BLK:(r+1)*BLK]=ring_ref[d,i*BLK:(i+1)*BLK,:].T
            else:
                a_ref[r*BLK:(r+1)*BLK,k*BLK:(k+1)*BLK]=ring_ref[d,i*BLK:(i+1)*BLK,:]
    y_ref[...]=jnp.zeros((n,n),jnp.float32)
    for x in range(1,planes):
        v_ref[:,(x-1)*BLK:x*BLK]=rhs_ref[x]
    zt_ref[...]=jnp.zeros(zt_ref.shape,jnp.float32)
    col_ref[...]=jnp.zeros((n,BLK),jnp.float32)
    rows=lax.broadcasted_iota(jnp.int32,(BLK,BLK),0); cols=lax.broadcasted_iota(jnp.int32,(BLK,BLK),1)
    eye=jnp.where(rows==cols,1.0,0.0).astype(jnp.float32)
    nv=(planes-1)*BLK
    def step(k,carry):
        for s in range(nblk):
            @pl.when(k==s)
            def _(s=s):
                m_ref[...]=a_ref[s*BLK:(s+1)*BLK,s*BLK:(s+1)*BLK]
        factor_block(m_ref[...],u_ref,m_ref)
        for s in range(nblk):
            @pl.when(k==s)
            def _(s=s):
                lo=s*BLK; hi=lo+BLK
                m=m_ref[...]
                parts=[]
                if s: parts.append(y_ref[lo:hi,:lo])
                if hi<n: parts.append(a_ref[lo:hi,hi:])
                parts.append(v_ref[lo:hi,:])
                full=mm(m,jnp.concatenate(parts,1))
                yk=jnp.concatenate([full[:,:lo],m],1) if s else m
                rest=full[:,lo:n-BLK]; vk=full[:,n-BLK:]
                if hi<n:
                    upd=mm(rest.T,jnp.concatenate([yk,rest,vk],1))
                    y_ref[hi:,:hi]-=upd[:,:hi]
                    a_ref[hi:,hi:]-=upd[:,hi:n]
                    v_ref[hi:,:]-=upd[:,n:]
                vt=jnp.concatenate([jnp.where(zpos==s,eye,0.0),vk],1).T
                zt_ref[:,:hi]+=mm(vt,yk)
                @pl.when(front==s)
                def _():
                    col_ref[lo:hi,:]=u_ref[...].T
                    for j in range(s+1,nblk):
                        col_ref[j*BLK:(j+1)*BLK,:]=rest[:,(j-s-1)*BLK:(j-s)*BLK].T
        return carry
    lax.fori_loop(0,nblk,step,0)

def child_factor(pos,ring,rhs):
    nblk=len(ring)-1; n=nblk*BLK; planes=rhs.shape[0]
    vm=pl.BlockSpec(memory_space=pltpu.VMEM)
    return pl.pallas_call(child_kernel,
        out_shape=(jax.ShapeDtypeStruct((planes*BLK,n),jnp.float32),jax.ShapeDtypeStruct((n,BLK),jnp.float32)),
        in_specs=[pl.BlockSpec(memory_space=pltpu.SMEM)]+[vm]*(nblk+2),
        out_specs=(vm,vm),
        scratch_shapes=[pltpu.VMEM((nblk,)+ring[0].shape,jnp.float32),pltpu.VMEM((n,n),jnp.float32),pltpu.VMEM((n,n),jnp.float32),pltpu.VMEM((n,(planes-1)*BLK),jnp.float32),pltpu.VMEM((BLK,BLK),jnp.float32),pltpu.VMEM((BLK,BLK),jnp.float32)],
        compiler_params=pltpu.CompilerParams(vmem_limit_bytes=30<<20),
        name="child_factor")(pos,*ring,rhs)


def split(a):
    hi=a.astype(jnp.bfloat16)
    return hi,(a-hi.astype(jnp.float32)).astype(jnp.bfloat16)

def mm3(a,b):
    ah,al=split(a); bh,bl=split(b)
    dot=lambda x,y: jnp.dot(x,y,preferred_element_type=jnp.float32)
    return dot(ah,bh)+(dot(ah,bl)+dot(al,bh))

UPD=2

def update_kernel(g_ref, zt_ref, out_ref, zh_ref, zl_ref):
    @pl.when(pl.program_id(0)==0)
    def _():
        zh,zl=split(zt_ref[...])
        zh_ref[...]=zh; zl_ref[...]=zl
    dot=lambda x,y: jnp.dot(x,y,preferred_element_type=jnp.float32)
    gh,gl=split(jnp.concatenate([g_ref[b] for b in range(UPD)],1))
    prod=dot(zh_ref[...],gh)+(dot(zh_ref[...],gl)+dot(zl_ref[...],gh))
    for x in range(out_ref.shape[0]):
        for b in range(UPD):
            out_ref[x,b*BLK:(b+1)*BLK,:]=prod[x*BLK:(x+1)*BLK,b*BLK:(b+1)*BLK].T

def child_update(gathered,zt):
    nblk,piv,_=gathered.shape; planes=zt.shape[0]//BLK
    return pl.pallas_call(update_kernel,
        out_shape=jax.ShapeDtypeStruct((planes,nblk*BLK,BLK),jnp.float32),
        grid=(nblk//UPD,),
        in_specs=[pl.BlockSpec((UPD,piv,BLK),lambda i:(i,0,0)),
            pl.BlockSpec(zt.shape,lambda i:(0,0))],
        out_specs=pl.BlockSpec((planes,UPD*BLK,BLK),lambda i:(0,i,0)),
        scratch_shapes=[pltpu.VMEM(zt.shape,jnp.bfloat16),pltpu.VMEM(zt.shape,jnp.bfloat16)],
        compiler_params=pltpu.CompilerParams(vmem_limit_bytes=24<<20),
        name="child_update")(gathered,zt)

def parent_kernel(pos_ref, p11_ref, wc_ref, p0_ref, p1_ref, p2_ref, p3_ref, par_ref, out_ref, u_ref, m_ref, wr_ref):
    front=pos_ref[0]; leaf=pos_ref[1]
    slots=wr_ref.shape[0]; cs=wc_ref.shape[0]
    xs=slots//cs; xpos=pos_ref[2]
    for d,ref in enumerate((p0_ref,p1_ref,p2_ref,p3_ref)):
        at=(xpos+d)%xs
        for c in range(cs):
            wr_ref[c*xs+at]=ref[c]
    a0=p11_ref[0]; a1=p11_ref[1]
    factor_block(a0[:BLK],u_ref,m_ref)
    m0=m_ref[...]; u00=u_ref[...]
    u01=mm(m0,a1[:BLK])
    u_ref[...]=a1[BLK:]-mm(u01.T,u01)
    factor_block(u_ref[...],u_ref,m_ref)
    m1=m_ref[...]; u11=u_ref[...]
    w=jnp.concatenate([wc_ref[c] for c in range(cs)]+[wr_ref[s] for s in range(slots)],1)
    v0=mm(m0,w[:BLK])
    v1=mm(m1,w[BLK:]-mm(u01.T,v0))
    v=jnp.concatenate([v0,v1],0)
    lrows=v[:,cs*BLK:].T
    prod=mm(lrows,v[:,:cs*BLK])
    for s in range(slots):
        for c in range(cs):
            at=pl.ds(s*BLK*cs+c,BLK,stride=cs)
            out_ref[at,:]=par_ref[at,:]-prod[s*BLK:(s+1)*BLK,c*BLK:(c+1)*BLK]
    for p in range(PARENT_PIVOTS):
        @pl.when(front==p)
        def _(p=p):
            for s in range(slots):
                out_ref[pl.ds(s*BLK*cs,BLK,stride=cs),:]=lrows[s*BLK:(s+1)*BLK,p*BLK:(p+1)*BLK]
    top0=pl.ds(0,BLK,stride=cs)
    zero=jnp.zeros((BLK,BLK),jnp.float32)
    @pl.when(leaf<PARENT_PIVOTS)
    def _():
        for c in range(1,cs):
            out_ref[pl.ds(c,BLK,stride=cs),:]=zero
        @pl.when(front>=PARENT_PIVOTS)
        def _():
            out_ref[top0,:]=zero
        @pl.when((front==0)&(leaf==0))
        def _():
            out_ref[top0,:]=u00.T
        @pl.when((front==1)&(leaf==1))
        def _():
            out_ref[top0,:]=u11.T
        @pl.when((front==1)&(leaf==0))
        def _():
            out_ref[top0,:]=zero

def parent_base(pos,p11,wc,planes,par):
    vm=pl.BlockSpec(memory_space=pltpu.VMEM)
    return pl.pallas_call(parent_kernel,
        out_shape=jax.ShapeDtypeStruct(par.shape,jnp.float32),
        in_specs=[pl.BlockSpec(memory_space=pltpu.SMEM)]+[vm]*(3+len(planes)),
        out_specs=vm,
        scratch_shapes=[pltpu.VMEM((BLK,BLK),jnp.float32),pltpu.VMEM((BLK,BLK),jnp.float32),pltpu.VMEM((len(planes)*wc.shape[0],)+wc.shape[1:],jnp.float32)],
        compiler_params=pltpu.CompilerParams(vmem_limit_bytes=20<<20),
        name="parent_base")(pos,p11,wc,*planes,par)

def extend_kernel(idx_ref, flag_ref, base_ref, recv_ref, out_ref):
    out_ref[...]=base_ref[...]
    groups,quota=recv_ref.shape[0],recv_ref.shape[1]
    cs=PARENT_CSLOTS
    @pl.when(flag_ref[0]>0)
    def _():
        for q in range(quota):
            for g in range(groups):
                start=idx_ref[q,g]
                at=pl.ds(start,BLK,stride=cs)
                out_ref[at,:]+=recv_ref[g,q]

def extend_add(idx,flag,base,recv):
    vm=pl.BlockSpec(memory_space=pltpu.VMEM); sm=pl.BlockSpec(memory_space=pltpu.SMEM)
    return pl.pallas_call(extend_kernel,
        out_shape=jax.ShapeDtypeStruct(base.shape,jnp.float32),
        in_specs=[sm,sm,vm,vm], out_specs=vm,
        input_output_aliases={2:0},
        compiler_params=pltpu.CompilerParams(vmem_limit_bytes=14<<20),
        name="extend_add")(idx,flag,base,recv)

def body(child_fronts, parent_front, child_map):
    XS,ZS=4,8
    leaf=lax.axis_index("leaf"); front=lax.axis_index("front")
    xpos=front//ZS; zpos=front%ZS
    own=child_fronts.reshape(child_fronts.shape[1],BLK)
    piv=CHILD_PIVOTS*BLK
    top=own[:piv]
    xg=[[x*ZS+z for x in range(XS)] for z in range(ZS)]
    zg=[[x*ZS+z for z in range(ZS)] for x in range(XS)]
    def fperm(pairs,v):
        return lax.ppermute(v,"front",pairs)
    def spread(v,groups):
        copies=jnp.broadcast_to(v[None],(len(groups[0]),)+v.shape)
        return lax.all_to_all(copies,"front",split_axis=0,concat_axis=0,tiled=True,axis_index_groups=groups)
    part=(CHILD_PIVOTS//2+1)*BLK
    piece=lax.dynamic_slice_in_dim(jnp.concatenate([top,top],0),zpos*BLK,part,0)
    mine=piece
    for d in range(1,XS):
        got=fperm([(z,d*ZS+z) for z in range(ZS)],piece)
        mine=jnp.where(xpos==d,got,mine)
    leaves=lax.axis_size("leaf")
    tie=lax.optimization_barrier
    def leaf_bcast(v):
        return lax.all_to_all(jnp.broadcast_to(v[None],(leaves,)+v.shape),"leaf",split_axis=0,concat_axis=0,tiled=True)
    both=("leaf","front")
    rel=(zpos-leaf)%ZS
    def relay(w,s):
        pairs=[(l*XS*ZS+x*ZS+(l+r)%ZS, l*XS*ZS+x*ZS+(l+r+s)%ZS) for l in range(ZS) for x in range(XS) for r in range(s)]
        got=lax.ppermute(w,both,pairs)
        return jnp.where((rel>=s)&(rel<2*s),got,w)
    prow=parent_front.reshape(parent_front.shape[0],BLK*PARENT_CSLOTS,BLK)
    rot=lambda d:[(x*ZS+z,x*ZS+(z+d)%ZS) for x in range(XS) for z in range(ZS)]
    ring=[None]*(ZS+1)
    mine,prow0,late=tie((mine,prow[0],top))
    ring[0]=mine
    fwd=fperm(rot(1),mine); bwd=fperm(rot(-1),mine)
    wc=leaf_bcast(prow0)[:PARENT_PIVOTS]
    rhs=spread(late,xg)
    wc=wc.reshape(PARENT_PIVOTS*BLK,PARENT_CSLOTS,BLK).transpose(1,0,2)
    fwd,bwd,wc=tie((fwd,bwd,wc))
    ring[ZS-1]=fwd; ring[1]=bwd
    fwd=fperm(rot(1),fwd); bwd=fperm(rot(-1),bwd); w=relay(wc,1)
    fwd,bwd,w=tie((fwd,bwd,w))
    ring[ZS-2]=fwd; ring[2]=bwd
    fwd=fperm(rot(1),fwd); bwd=fperm(rot(-1),bwd); w=relay(w,2)
    fwd,bwd,w=tie((fwd,bwd,w))
    ring[ZS-3]=fwd; ring[3]=bwd
    half=part//2
    fwd=fperm(rot(1),fwd[:half]); bwd=fperm(rot(-1),bwd[half:]); w=relay(w,4)
    fwd,bwd,w,late=tie((fwd,bwd,w,late))
    ring[ZS//2]=fwd; ring[ZS]=bwd
    gathered=spread(late,zg)
    planes=[w]
    for d in range(1,XS):
        planes.append(fperm([(x*ZS+z,((x-d)%XS)*ZS+z) for x in range(XS) for z in range(ZS)],w))
    pos=jnp.stack([front,zpos]).astype(jnp.int32)
    zt,col=child_factor(pos,ring,rhs)
    pivot=planes[0][0]
    for d in range(1,XS):
        pivot=jnp.where(xpos==XS-d,planes[d][0],pivot)
    zt,gathered,pivot=tie((zt,gathered,pivot))
    p11=leaf_bcast(pivot)[:PARENT_PIVOTS]
    prod=child_update(gathered,zt)
    prod=lax.all_to_all(prod,"front",split_axis=0,concat_axis=0,tiled=True,axis_index_groups=xg)
    prod=prod[1:].reshape(own.shape[0]-piv,BLK)
    out=jnp.concatenate([col,jnp.where(xpos==0,prod,own[piv:]-prod)],0)
    quota=(own.shape[0]-piv)//BLK//leaves
    blocks=(quota,leaves,BLK,BLK)
    sent=jnp.where(xpos==0,prod.reshape(blocks),own[piv:].reshape(blocks)-prod.reshape(blocks)).transpose(1,0,2,3)
    sent,p11=tie((sent,p11))
    recv=lax.all_to_all(sent,"leaf",split_axis=0,concat_axis=0,tiled=True)
    base=parent_base(jnp.stack([front,leaf,xpos]).astype(jnp.int32),p11,wc,planes,prow.reshape(-1,BLK))
    rowsel=(jnp.arange(leaves)==leaf)
    rmap=jnp.sum(jnp.where(rowsel[None,None,:],child_map.reshape(leaves,quota,leaves),0),axis=2)
    vblk=front-CHILD_PIVOTS
    csel=(jnp.arange(child_map.shape[1])==vblk)
    cmap=jnp.sum(jnp.where(csel[None,:],child_map,0),axis=1)
    idx=((rmap//leaves)*(BLK*PARENT_CSLOTS)+(cmap//32)[:,None]).T.astype(jnp.int32)
    flag=(front>=CHILD_PIVOTS).astype(jnp.int32).reshape(1)
    parent=extend_add(idx,flag,base,recv)
    return out.reshape(child_fronts.shape),parent.reshape(parent_front.shape)


def solution(mesh):
    return jax.shard_map(
        body,
        mesh=mesh,
        in_specs=(
            P("leaf", None, None, "front", None),
            P(None, "leaf", None, None, "front", None),
            P(),
        ),
        out_specs=(
            P("leaf", None, None, "front", None),
            P(None, "leaf", None, None, "front", None),
        ),
        check_vma=False,
    )
```

```python
import jax, jax.numpy as jnp
from jax import lax
from jax.experimental import pallas as pl
from jax.experimental.pallas import tpu as pltpu
from jax.sharding import PartitionSpec as P

BLK=128
CHILD_PIVOTS=8
PARENT_PIVOTS=2
PARENT_CSLOTS=2
NB=16
HI=lax.Precision.HIGHEST

def mm(a,b):
    return jnp.dot(a,b,precision=HI,preferred_element_type=jnp.float32)

def split(a):
    hi=a.astype(jnp.bfloat16)
    return hi,(a-hi.astype(jnp.float32)).astype(jnp.bfloat16)

def mm3(a,b):
    ah,al=split(a); bh,bl=split(b)
    dot=lambda x,y: jnp.dot(x,y,preferred_element_type=jnp.float32)
    return dot(ah,bh)+(dot(ah,bl)+dot(al,bh))

def factor_block(a, u_ref, m_ref, nb=None):
    nb = nb or NB
    n=BLK
    rows=lax.broadcasted_iota(jnp.int32,(n,n),0); cols=lax.broadcasted_iota(jnp.int32,(n,n),1)
    inv=jnp.where(rows==cols,1.0,0.0).astype(jnp.float32)
    sub=lax.broadcasted_iota(jnp.int32,(nb,n),0)
    lane=lax.broadcasted_iota(jnp.int32,(nb,n),1)
    for c0 in range(0,n,nb):
        r=a[c0:c0+nb,:]; y=inv[c0:c0+nb,:]
        bc=[jnp.broadcast_to(r[:,c0+t:c0+t+1],(nb,n)) for t in range(nb)]
        piv=jnp.ones((nb,n),jnp.float32)
        for t in range(nb):
            p=jnp.broadcast_to(bc[t][t:t+1,:],(nb,n))
            piv=jnp.where(sub==t,p,piv)
            if t==nb-1: break
            m=jnp.where(sub>t,bc[t]*(1.0/p),0.0)
            for q in range(t+1,nb):
                bc[q]=bc[q]-m*jnp.broadcast_to(bc[q][t:t+1,:],(nb,n))
            r=r-m*jnp.broadcast_to(r[t:t+1,:],(nb,n))
            y=y-m*jnp.broadcast_to(y[t:t+1,:],(nb,n))
        scale=lax.rsqrt(piv)
        u=jnp.where(lane>=sub+c0,r*scale,0.0); y=y*scale
        u_ref[c0:c0+nb,:]=u; m_ref[c0:c0+nb,:]=y
        if c0+nb<n:
            upd=mm(u.T,jnp.concatenate([u,y],1))
            a=a-upd[:,:n]; inv=inv-upd[:,n:]

def child_kernel(pos_ref, q0_ref, q1_ref, q2_ref, q3_ref, yt_ref, col_ref, ring_ref, a_ref, u_ref, m_ref):
    front=pos_ref[0]; xpos=pos_ref[2]; nblk,prow,_=q0_ref.shape; n=BLK*nblk; half=nblk//2
    refs=(q0_ref,q1_ref,q2_ref,q3_ref)
    for d,ref in enumerate(refs):
        at=pl.multiple_of(((xpos+d)%len(refs))*prow,8)
        for k in range(nblk):
            ring_ref[k,pl.ds(at,prow),:]=ref[k]
    for k in range(nblk):
        for i in range(half+1):
            r=(k+i)%nblk
            if r>k:
                if i<half: a_ref[k*BLK:(k+1)*BLK,r*BLK:(r+1)*BLK]=ring_ref[k,i*BLK:(i+1)*BLK,:].T
            else:
                a_ref[r*BLK:(r+1)*BLK,k*BLK:(k+1)*BLK]=ring_ref[k,i*BLK:(i+1)*BLK,:]
    y_ref=yt_ref
    y_ref[...]=jnp.zeros((n,n),jnp.float32)
    col_ref[...]=jnp.zeros((n,BLK),jnp.float32)
    def step(k,carry):
        for s in range(nblk):
            @pl.when(k==s)
            def _(s=s):
                m_ref[...]=a_ref[s*BLK:(s+1)*BLK,s*BLK:(s+1)*BLK]
        factor_block(m_ref[...],u_ref,m_ref)
        for s in range(nblk):
            @pl.when(k==s)
            def _(s=s):
                lo=s*BLK; hi=lo+BLK
                m=m_ref[...]
                parts=[]
                if s: parts.append(y_ref[lo:hi,:lo])
                if hi<n: parts.append(a_ref[lo:hi,hi:])
                full=mm(m,jnp.concatenate(parts,1))
                yk=jnp.concatenate([full[:,:lo],m],1) if s else m
                y_ref[lo:hi,:hi]=yk
                rest=full[:,lo:]
                if hi<n:
                    upd=mm(rest.T,jnp.concatenate([yk,rest],1))
                    y_ref[hi:,:hi]-=upd[:,:hi]
                    a_ref[hi:,hi:]-=upd[:,hi:n]
                @pl.when(front==s)
                def _():
                    col_ref[lo:hi,:]=u_ref[...].T
                    for j in range(s+1,nblk):
                        col_ref[j*BLK:(j+1)*BLK,:]=rest[:,(j-s-1)*BLK:(j-s)*BLK].T
        return carry
    lax.fori_loop(0,nblk,step,0)

def child_factor(pos,parts):
    nblk,prow,_=parts[0].shape; n=nblk*BLK; quarters=len(parts)
    vm=pl.BlockSpec(memory_space=pltpu.VMEM)
    return pl.pallas_call(child_kernel,
        out_shape=(jax.ShapeDtypeStruct((n,n),jnp.float32),jax.ShapeDtypeStruct((n,BLK),jnp.float32)),
        in_specs=[pl.BlockSpec(memory_space=pltpu.SMEM)]+[vm]*quarters,
        out_specs=(vm,vm),
        scratch_shapes=[pltpu.VMEM((nblk,quarters*prow,BLK),jnp.float32),pltpu.VMEM((n,n),jnp.float32),pltpu.VMEM((BLK,BLK),jnp.float32),pltpu.VMEM((BLK,BLK),jnp.float32)],
        compiler_params=pltpu.CompilerParams(vmem_limit_bytes=30<<20),
        name="child_factor")(pos,*parts)


UPD=2

def update_kernel(pos_ref, g_ref, y_ref, f0_ref, f1_ref, f2_ref, f3_ref, o0_ref, o1_ref, o2_ref, o3_ref, zh_ref, zl_ref):
    zpos=pos_ref[1]; xpos=pos_ref[2]; outs=(o0_ref,o1_ref,o2_ref,o3_ref); planes=len(outs)
    dot=lambda x,y: jnp.dot(x,y,preferred_element_type=jnp.float32)
    @pl.when(pl.program_id(0)==0)
    def _():
        yh,yl=split(y_ref[...])
        fh,fl=split(jnp.concatenate([r[...] for r in (f0_ref,f1_ref,f2_ref,f3_ref)],1))
        v=dot(yh,fh)+(dot(yh,fl)+dot(yl,fh))
        vh,vl=split(v.T)
        zt=dot(vh,yh)+(dot(vh,yl)+dot(vl,yh))
        zh,zl=split(zt)
        zh_ref[...]=zh; zl_ref[...]=zl
        zh,zl=split(y_ref[pl.ds(pl.multiple_of(zpos*BLK,BLK),BLK),:])
        for d in range(planes):
            @pl.when((xpos+d)%planes==0)
            def _(d=d):
                zh_ref[d*BLK:(d+1)*BLK]=zh; zl_ref[d*BLK:(d+1)*BLK]=zl
    gh,gl=split(jnp.concatenate([g_ref[b] for b in range(UPD)],1))
    prod=dot(zh_ref[...],gh)+(dot(zh_ref[...],gl)+dot(zl_ref[...],gh))
    for d in range(planes):
        for b in range(UPD):
            outs[d][b*BLK:(b+1)*BLK,:]=prod[d*BLK:(d+1)*BLK,b*BLK:(b+1)*BLK].T

def child_update(pos,gathered,y,rhs):
    nblk,piv,_=gathered.shape; planes=len(rhs)
    vm=pl.BlockSpec(memory_space=pltpu.VMEM)
    return pl.pallas_call(update_kernel,
        out_shape=(jax.ShapeDtypeStruct((nblk*BLK,BLK),jnp.float32),)*planes,
        grid=(nblk//UPD,),
        in_specs=[pl.BlockSpec(memory_space=pltpu.SMEM),pl.BlockSpec((UPD,piv,BLK),lambda i:(i,0,0))]+[vm]*(1+planes),
        out_specs=(pl.BlockSpec((UPD*BLK,BLK),lambda i:(i,0)),)*planes,
        scratch_shapes=[pltpu.VMEM((planes*BLK,piv),jnp.bfloat16),pltpu.VMEM((planes*BLK,piv),jnp.bfloat16)],
        compiler_params=pltpu.CompilerParams(vmem_limit_bytes=36<<20),
        name="child_update")(pos,gathered,y,*rhs)

def combine_kernel(pos_ref, r0_ref, r1_ref, r2_ref, r3_ref, own_ref, col_ref, out_ref, sent_ref):
    xpos=pos_ref[2]; refs=(r0_ref,r1_ref,r2_ref,r3_ref); planes=len(refs)
    head=col_ref.shape[0]; nblk=r0_ref.shape[0]//BLK
    out_ref[:head,:]=col_ref[...]
    for d,ref in enumerate(refs):
        src=(xpos-d+planes)%planes
        @pl.when(src>0)
        def _(ref=ref,src=src):
            for j in range(nblk):
                at=pl.multiple_of(src*head+j*BLK,BLK)
                r=ref[j*BLK:(j+1)*BLK,:]
                val=jnp.where(xpos==0,r,own_ref[pl.ds(at,BLK),:]-r)
                out_ref[pl.ds(at,BLK),:]=val
                sent_ref[j,src-1]=val

def combine(pos,parts,own,col):
    vm=pl.BlockSpec(memory_space=pltpu.VMEM); nblk=parts[0].shape[0]//BLK
    return pl.pallas_call(combine_kernel,
        out_shape=(jax.ShapeDtypeStruct(own.shape,jnp.float32),jax.ShapeDtypeStruct((nblk,len(parts)-1,BLK,BLK),jnp.float32)),
        in_specs=[pl.BlockSpec(memory_space=pltpu.SMEM)]+[vm]*(2+len(parts)),
        out_specs=(vm,vm),
        compiler_params=pltpu.CompilerParams(vmem_limit_bytes=14<<20),
        name="combine")(pos,*parts,own,col)

def parent_kernel(pos_ref, all_ref, wc_ref, par_ref, out_ref, u_ref, m_ref, wr_ref, p11_ref):
    front=pos_ref[0]; leaf=pos_ref[1]
    slots=wr_ref.shape[0]; cs=wc_ref.shape[0]; xs=slots//cs
    for f in range(all_ref.shape[0]):
        for t in range(slots):
            wr_ref[(t%cs)*xs+t//cs,8*f:8*f+8,:]=all_ref[f,t]
        for p in range(PARENT_PIVOTS):
            p11_ref[p,8*f:8*f+8,:]=all_ref[f,slots+p]
    a0=p11_ref[0]; a1=p11_ref[1]
    factor_block(a0[:BLK],u_ref,m_ref)
    m0=m_ref[...]; u00=u_ref[...]
    u01=mm(m0,a1[:BLK])
    u_ref[...]=a1[BLK:]-mm(u01.T,u01)
    factor_block(u_ref[...],u_ref,m_ref)
    m1=m_ref[...]; u11=u_ref[...]
    w=jnp.concatenate([wc_ref[c] for c in range(cs)]+[wr_ref[s] for s in range(slots)],1)
    v0=mm(m0,w[:BLK])
    v1=mm(m1,w[BLK:]-mm(u01.T,v0))
    v=jnp.concatenate([v0,v1],0)
    lrows=v[:,cs*BLK:].T
    prod=mm(lrows,v[:,:cs*BLK])
    for s in range(slots):
        for c in range(cs):
            at=pl.ds(s*BLK*cs+c,BLK,stride=cs)
            out_ref[at,:]=par_ref[at,:]-prod[s*BLK:(s+1)*BLK,c*BLK:(c+1)*BLK]
    for p in range(PARENT_PIVOTS):
        @pl.when(front==p)
        def _(p=p):
            for s in range(slots):
                out_ref[pl.ds(s*BLK*cs,BLK,stride=cs),:]=lrows[s*BLK:(s+1)*BLK,p*BLK:(p+1)*BLK]
    top0=pl.ds(0,BLK,stride=cs)
    zero=jnp.zeros((BLK,BLK),jnp.float32)
    @pl.when(leaf<PARENT_PIVOTS)
    def _():
        for c in range(1,cs):
            out_ref[pl.ds(c,BLK,stride=cs),:]=zero
        @pl.when(front>=PARENT_PIVOTS)
        def _():
            out_ref[top0,:]=zero
        @pl.when((front==0)&(leaf==0))
        def _():
            out_ref[top0,:]=u00.T
        @pl.when((front==1)&(leaf==1))
        def _():
            out_ref[top0,:]=u11.T
        @pl.when((front==1)&(leaf==0))
        def _():
            out_ref[top0,:]=zero

def parent_base(pos,everything,wc,par):
    vm=pl.BlockSpec(memory_space=pltpu.VMEM)
    cs,rows,_=wc.shape; slots=everything.shape[1]-PARENT_PIVOTS
    return pl.pallas_call(parent_kernel,
        out_shape=jax.ShapeDtypeStruct(par.shape,jnp.float32),
        in_specs=[pl.BlockSpec(memory_space=pltpu.SMEM),vm,vm,vm],
        out_specs=vm,
        scratch_shapes=[pltpu.VMEM((BLK,BLK),jnp.float32),pltpu.VMEM((BLK,BLK),jnp.float32),
            pltpu.VMEM((slots,rows,BLK),jnp.float32),pltpu.VMEM((PARENT_PIVOTS,rows,BLK),jnp.float32)],
        compiler_params=pltpu.CompilerParams(vmem_limit_bytes=20<<20),
        name="parent_base")(pos,everything,wc,par)

def extend_kernel(idx_ref, flag_ref, base_ref, recv_ref, out_ref):
    out_ref[...]=base_ref[...]
    groups,quota=recv_ref.shape[0],recv_ref.shape[1]
    cs=PARENT_CSLOTS
    @pl.when(flag_ref[0]>0)
    def _():
        for q in range(quota):
            for g in range(groups):
                start=idx_ref[q,g]
                at=pl.ds(start,BLK,stride=cs)
                out_ref[at,:]+=recv_ref[g,q]

def extend_add(idx,flag,base,recv):
    vm=pl.BlockSpec(memory_space=pltpu.VMEM); sm=pl.BlockSpec(memory_space=pltpu.SMEM)
    return pl.pallas_call(extend_kernel,
        out_shape=jax.ShapeDtypeStruct(base.shape,jnp.float32),
        in_specs=[sm,sm,vm,vm], out_specs=vm,
        input_output_aliases={2:0},
        compiler_params=pltpu.CompilerParams(vmem_limit_bytes=14<<20),
        name="extend_add")(idx,flag,base,recv)

def body(child_fronts, parent_front, child_map):
    XS,ZS=4,8
    leaf=lax.axis_index("leaf"); front=lax.axis_index("front")
    xpos=front//ZS; zpos=front%ZS
    own=child_fronts.reshape(child_fronts.shape[1],BLK)
    piv=CHILD_PIVOTS*BLK
    top=own[:piv]
    xg=[[x*ZS+z for x in range(XS)] for z in range(ZS)]
    zg=[[x*ZS+z for z in range(ZS)] for x in range(XS)]
    def spread(v,groups):
        copies=jnp.broadcast_to(v[None],(len(groups[0]),)+v.shape)
        return lax.all_to_all(copies,"front",split_axis=0,concat_axis=0,tiled=True,axis_index_groups=groups)
    leaves=lax.axis_size("leaf"); fronts=XS*ZS
    tie=lax.optimization_barrier
    def swap(v,axis,groups=None):
        return lax.all_to_all(v,axis,split_axis=0,concat_axis=0,tiled=True,axis_index_groups=groups)
    def copies(v,n):
        return jnp.broadcast_to(v[None],(n,)+v.shape)
    part=(CHILD_PIVOTS//2+1)*BLK
    piece=lax.dynamic_slice_in_dim(jnp.concatenate([top,top],0),zpos*BLK,part,0)
    def hop(d):
        return [(x*ZS+z,((x+d)%XS)*ZS+z) for x in range(XS) for z in range(ZS)]
    def fperm(pairs,v):
        return lax.ppermute(v,"front",pairs)
    quarters=piece.reshape(XS,part//XS,BLK)
    piece=quarters[0]
    for d in range(1,XS):
        piece=jnp.where(xpos==d,fperm([(z,d*ZS+z) for z in range(ZS)],quarters[d]),piece)
    prow=parent_front.reshape(parent_front.shape[0],BLK*PARENT_CSLOTS,BLK)
    wc=swap(copies(prow[0],leaves),"leaf")[:PARENT_PIVOTS]
    piece,top1,wc=tie((piece,top,wc))
    quarter=swap(copies(piece,ZS),"front",zg)
    rhs=[top1]+[fperm(hop(-d),top1) for d in range(1,XS)]
    wc=wc.reshape(PARENT_PIVOTS*BLK,PARENT_CSLOTS,BLK).transpose(1,0,2)
    quarter,top2,*rhs=tie((quarter,top1,*rhs))
    parts=[quarter]+[fperm(hop(-d),quarter) for d in range(1,XS)]
    gathered=spread(top2,zg)
    pos=jnp.stack([front,zpos,xpos]).astype(jnp.int32)
    y,col=child_factor(pos,parts)
    gathered,wc,y=tie((gathered,wc,y))
    eighth=wc.reshape(PARENT_CSLOTS,fronts,8,BLK).transpose(1,0,2,3)
    got=swap(eighth,"front")
    mine=lax.dynamic_index_in_dim(got.reshape(XS,ZS,PARENT_CSLOTS,8,BLK),leaf,axis=1,keepdims=False)
    mine=jnp.concatenate([mine.reshape(XS*PARENT_CSLOTS,8,BLK),got[:PARENT_PIVOTS,0]],0)
    *prods,mine=tie((*child_update(pos,gathered,y,rhs),mine))
    everything=swap(copies(mine,fronts),"front")
    prods=[prods[0]]+[fperm(hop(d),prods[d]) for d in range(1,XS)]
    out,sent=combine(pos,prods,own,col)
    quota=(own.shape[0]-piv)//BLK//leaves
    sent,everything=tie((sent,everything))
    recv=lax.all_to_all(sent,"leaf",split_axis=0,concat_axis=0,tiled=True)
    base=parent_base(jnp.stack([front,leaf]).astype(jnp.int32),everything,wc,prow.reshape(-1,BLK))
    rowsel=(jnp.arange(leaves)==leaf)
    rmap=jnp.sum(jnp.where(rowsel[None,None,:],child_map.reshape(leaves,quota,leaves),0),axis=2)
    vblk=front-CHILD_PIVOTS
    csel=(jnp.arange(child_map.shape[1])==vblk)
    cmap=jnp.sum(jnp.where(csel[None,:],child_map,0),axis=1)
    idx=((rmap//leaves)*(BLK*PARENT_CSLOTS)+(cmap//32)[:,None]).T.astype(jnp.int32)
    flag=(front>=CHILD_PIVOTS).astype(jnp.int32).reshape(1)
    parent=extend_add(idx,flag,base,recv)
    return out.reshape(child_fronts.shape),parent.reshape(parent_front.shape)


def solution(mesh):
    return jax.shard_map(
        body,
        mesh=mesh,
        in_specs=(
            P("leaf", None, None, "front", None),
            P(None, "leaf", None, None, "front", None),
            P(),
        ),
        out_specs=(
            P("leaf", None, None, "front", None),
            P(None, "leaf", None, None, "front", None),
        ),
        check_vma=False,
    )
```

```python
import jax, jax.numpy as jnp
from jax import lax
from jax.experimental import pallas as pl
from jax.experimental.pallas import tpu as pltpu
from jax.sharding import PartitionSpec as P

BLK=128
CHILD_PIVOTS=8
PARENT_PIVOTS=2
PARENT_CSLOTS=2
NB=16
HI=lax.Precision.HIGHEST

def mm(a,b):
    return jnp.dot(a,b,precision=HI,preferred_element_type=jnp.float32)

def split(a):
    hi=a.astype(jnp.bfloat16)
    return hi,(a-hi.astype(jnp.float32)).astype(jnp.bfloat16)

def mm3(a,b):
    ah,al=split(a); bh,bl=split(b)
    dot=lambda x,y: jnp.dot(x,y,preferred_element_type=jnp.float32)
    return dot(ah,bh)+(dot(ah,bl)+dot(al,bh))

def factor_block(a, u_ref, m_ref, nb=None):
    nb = nb or NB
    n=BLK
    rows=lax.broadcasted_iota(jnp.int32,(n,n),0); cols=lax.broadcasted_iota(jnp.int32,(n,n),1)
    inv=jnp.where(rows==cols,1.0,0.0).astype(jnp.float32)
    sub=lax.broadcasted_iota(jnp.int32,(nb,n),0)
    lane=lax.broadcasted_iota(jnp.int32,(nb,n),1)
    for c0 in range(0,n,nb):
        r=a[c0:c0+nb,:]; y=inv[c0:c0+nb,:]
        bc=[jnp.broadcast_to(r[:,c0+t:c0+t+1],(nb,n)) for t in range(nb)]
        piv=jnp.ones((nb,n),jnp.float32)
        for t in range(nb):
            p=jnp.broadcast_to(bc[t][t:t+1,:],(nb,n))
            piv=jnp.where(sub==t,p,piv)
            if t==nb-1: break
            m=jnp.where(sub>t,bc[t]*(1.0/p),0.0)
            for q in range(t+1,nb):
                bc[q]=bc[q]-m*jnp.broadcast_to(bc[q][t:t+1,:],(nb,n))
            r=r-m*jnp.broadcast_to(r[t:t+1,:],(nb,n))
            y=y-m*jnp.broadcast_to(y[t:t+1,:],(nb,n))
        scale=lax.rsqrt(piv)
        u=jnp.where(lane>=sub+c0,r*scale,0.0); y=y*scale
        u_ref[c0:c0+nb,:]=u; m_ref[c0:c0+nb,:]=y
        if c0+nb<n:
            upd=mm(u.T,jnp.concatenate([u,y],1))
            a=a-upd[:,:n]; inv=inv-upd[:,n:]

def child_kernel(pos_ref, q0_ref, q1_ref, q2a_ref, q2b_ref, q3_ref, yt_ref, col_ref, ring_ref, a_ref, u_ref, m_ref):
    front=pos_ref[0]; xpos=pos_ref[2]; nblk,prow,_=q0_ref.shape; n=BLK*nblk; half=nblk//2
    for d,first,ref in ((0,0,q0_ref),(1,0,q1_ref),(2,0,q2a_ref),(2,nblk//2,q2b_ref),(3,0,q3_ref)):
        at=pl.multiple_of(((xpos+d)%4)*prow,8)
        for k in range(ref.shape[0]):
            ring_ref[first+k,pl.ds(at,prow),:]=ref[k]
    for k in range(nblk):
        for i in range(half+1):
            r=(k+i)%nblk
            if r>k:
                if i<half: a_ref[k*BLK:(k+1)*BLK,r*BLK:(r+1)*BLK]=ring_ref[k,i*BLK:(i+1)*BLK,:].T
            else:
                a_ref[r*BLK:(r+1)*BLK,k*BLK:(k+1)*BLK]=ring_ref[k,i*BLK:(i+1)*BLK,:]
    y_ref=yt_ref
    y_ref[...]=jnp.zeros((n,n),jnp.float32)
    col_ref[...]=jnp.zeros((n,BLK),jnp.float32)
    def step(k,carry):
        for s in range(nblk):
            @pl.when(k==s)
            def _(s=s):
                m_ref[...]=a_ref[s*BLK:(s+1)*BLK,s*BLK:(s+1)*BLK]
        factor_block(m_ref[...],u_ref,m_ref)
        for s in range(nblk):
            @pl.when(k==s)
            def _(s=s):
                lo=s*BLK; hi=lo+BLK
                m=m_ref[...]
                parts=[]
                if s: parts.append(y_ref[lo:hi,:lo])
                if hi<n: parts.append(a_ref[lo:hi,hi:])
                full=mm(m,jnp.concatenate(parts,1))
                yk=jnp.concatenate([full[:,:lo],m],1) if s else m
                y_ref[lo:hi,:hi]=yk
                rest=full[:,lo:]
                if hi<n:
                    upd=mm(rest.T,jnp.concatenate([yk,rest],1))
                    y_ref[hi:,:hi]-=upd[:,:hi]
                    a_ref[hi:,hi:]-=upd[:,hi:n]
                @pl.when(front==s)
                def _():
                    col_ref[lo:hi,:]=u_ref[...].T
                    for j in range(s+1,nblk):
                        col_ref[j*BLK:(j+1)*BLK,:]=rest[:,(j-s-1)*BLK:(j-s)*BLK].T
        return carry
    lax.fori_loop(0,nblk,step,0)

def child_factor(pos,parts):
    nblk,prow,_=parts[0].shape; n=nblk*BLK; quarters=len(parts)-1
    vm=pl.BlockSpec(memory_space=pltpu.VMEM)
    return pl.pallas_call(child_kernel,
        out_shape=(jax.ShapeDtypeStruct((n,n),jnp.float32),jax.ShapeDtypeStruct((n,BLK),jnp.float32)),
        in_specs=[pl.BlockSpec(memory_space=pltpu.SMEM)]+[vm]*len(parts),
        out_specs=(vm,vm),
        scratch_shapes=[pltpu.VMEM((nblk,quarters*prow,BLK),jnp.float32),pltpu.VMEM((n,n),jnp.float32),pltpu.VMEM((BLK,BLK),jnp.float32),pltpu.VMEM((BLK,BLK),jnp.float32)],
        compiler_params=pltpu.CompilerParams(vmem_limit_bytes=30<<20),
        name="child_factor")(pos,*parts)


UPD=2

def update_kernel(pos_ref, after_ref, *refs):
    g=refs[:7]; y_ref=refs[7]; f=refs[8:9]; outs=refs[9:13]; zh_ref,zl_ref=refs[13:]
    n=y_ref.shape[0]
    zpos=pos_ref[1]; xpos=pos_ref[2]; planes=len(outs)
    dot=lambda x,y: jnp.dot(x,y,preferred_element_type=jnp.float32)
    yh,yl=split(y_ref[...])
    fh,fl=split(jnp.concatenate([f[0][(xpos+d)%planes] for d in range(planes)],1))
    v=dot(yh,fh)+(dot(yh,fl)+dot(yl,fh))
    vh,vl=split(v.T)
    zt=dot(vh,yh)+(dot(vh,yl)+dot(vl,yh))
    zh,zl=split(zt)
    zh_ref[...]=zh; zl_ref[...]=zl
    zh,zl=split(y_ref[pl.ds(pl.multiple_of(zpos*BLK,BLK),BLK),:])
    for d in range(planes):
        @pl.when((xpos+d)%planes==0)
        def _(d=d):
            zh_ref[d*BLK:(d+1)*BLK]=zh; zl_ref[d*BLK:(d+1)*BLK]=zl
    blocks=[r[:n,:] for r in g]
    blocks.insert(4,jnp.concatenate([g[4][n:,:],g[3][n:,:]],0))
    for d in range(0,len(blocks),2):
        gh,gl=split(jnp.concatenate(blocks[d:d+2],1))
        prod=dot(zh_ref[...],gh)+(dot(zh_ref[...],gl)+dot(zl_ref[...],gh))
        for x in range(planes):
            for b in range(2):
                outs[x][(d+b)*BLK:(d+b+1)*BLK,:]=prod[x*BLK:(x+1)*BLK,b*BLK:(b+1)*BLK].T

def child_update(pos,after,gathered,y,rhs):
    piv=y.shape[0]; planes=rhs.shape[0]
    vm=pl.BlockSpec(memory_space=pltpu.VMEM)
    return pl.pallas_call(update_kernel,
        out_shape=(jax.ShapeDtypeStruct((piv,BLK),jnp.float32),)*planes,
        in_specs=[pl.BlockSpec(memory_space=pltpu.SMEM)]+[vm]*(len(gathered)+3),
        out_specs=(vm,)*planes,
        scratch_shapes=[pltpu.VMEM((planes*BLK,piv),jnp.bfloat16),pltpu.VMEM((planes*BLK,piv),jnp.bfloat16)],
        compiler_params=pltpu.CompilerParams(vmem_limit_bytes=40<<20),
        name="child_update")(pos,after,*gathered,y,rhs)

def combine_kernel(pos_ref, r0_ref, r1_ref, r2a_ref, r2b_ref, r3_ref, own_ref, col_ref, out_ref, sent_ref):
    zpos=pos_ref[1]; xpos=pos_ref[2]
    head=col_ref.shape[0]; nblk=r0_ref.shape[0]//BLK
    out_ref[:head,:]=col_ref[...]
    for d,first,ref in ((0,0,r0_ref),(1,0,r1_ref),(2,0,r2a_ref),(2,nblk//2,r2b_ref),(3,0,r3_ref)):
        src=(xpos-d+4)%4
        @pl.when(src>0)
        def _(first=first,ref=ref,src=src):
            for j in range(ref.shape[0]//BLK):
                blk=(zpos+first+j)%nblk
                at=pl.multiple_of(src*head+blk*BLK,BLK)
                r=ref[j*BLK:(j+1)*BLK,:]
                val=jnp.where(xpos==0,r,own_ref[pl.ds(at,BLK),:]-r)
                out_ref[pl.ds(at,BLK),:]=val
                sent_ref[blk,src-1]=val

def combine(pos,parts,own,col):
    vm=pl.BlockSpec(memory_space=pltpu.VMEM); nblk=parts[0].shape[0]//BLK
    return pl.pallas_call(combine_kernel,
        out_shape=(jax.ShapeDtypeStruct(own.shape,jnp.float32),jax.ShapeDtypeStruct((nblk,len(parts)-2,BLK,BLK),jnp.float32)),
        in_specs=[pl.BlockSpec(memory_space=pltpu.SMEM)]+[vm]*(2+len(parts)),
        out_specs=(vm,vm),
        compiler_params=pltpu.CompilerParams(vmem_limit_bytes=14<<20),
        name="combine")(pos,*parts,own,col)

def parent_kernel(pos_ref, e0_ref, e1_ref, e2_ref, e3_ref, wc_ref, par_ref, out_ref, u_ref, m_ref, wr_ref, p11_ref):
    front=pos_ref[0]; leaf=pos_ref[1]; xpos=pos_ref[2]
    slots=wr_ref.shape[0]; cs=wc_ref.shape[0]; xs=slots//cs
    for d,ref in enumerate((e0_ref,e1_ref,e2_ref,e3_ref)):
        for z in range(ref.shape[0]):
            at=pl.ds(pl.multiple_of(((xpos+d)%xs)*8*ref.shape[0]+8*z,8),8)
            for t in range(slots):
                wr_ref[(t%cs)*xs+t//cs,at,:]=ref[z,t]
            for p in range(PARENT_PIVOTS):
                p11_ref[p,at,:]=ref[z,slots+p]
    a0=p11_ref[0]; a1=p11_ref[1]
    factor_block(a0[:BLK],u_ref,m_ref)
    m0=m_ref[...]; u00=u_ref[...]
    u01=mm(m0,a1[:BLK])
    u_ref[...]=a1[BLK:]-mm(u01.T,u01)
    factor_block(u_ref[...],u_ref,m_ref)
    m1=m_ref[...]; u11=u_ref[...]
    w=jnp.concatenate([wc_ref[c] for c in range(cs)]+[wr_ref[s] for s in range(slots)],1)
    v0=mm(m0,w[:BLK])
    v1=mm(m1,w[BLK:]-mm(u01.T,v0))
    v=jnp.concatenate([v0,v1],0)
    lrows=v[:,cs*BLK:].T
    prod=mm(lrows,v[:,:cs*BLK])
    for s in range(slots):
        for c in range(cs):
            at=pl.ds(s*BLK*cs+c,BLK,stride=cs)
            out_ref[at,:]=par_ref[at,:]-prod[s*BLK:(s+1)*BLK,c*BLK:(c+1)*BLK]
    for p in range(PARENT_PIVOTS):
        @pl.when(front==p)
        def _(p=p):
            for s in range(slots):
                out_ref[pl.ds(s*BLK*cs,BLK,stride=cs),:]=lrows[s*BLK:(s+1)*BLK,p*BLK:(p+1)*BLK]
    top0=pl.ds(0,BLK,stride=cs)
    zero=jnp.zeros((BLK,BLK),jnp.float32)
    @pl.when(leaf<PARENT_PIVOTS)
    def _():
        for c in range(1,cs):
            out_ref[pl.ds(c,BLK,stride=cs),:]=zero
        @pl.when(front>=PARENT_PIVOTS)
        def _():
            out_ref[top0,:]=zero
        @pl.when((front==0)&(leaf==0))
        def _():
            out_ref[top0,:]=u00.T
        @pl.when((front==1)&(leaf==1))
        def _():
            out_ref[top0,:]=u11.T
        @pl.when((front==1)&(leaf==0))
        def _():
            out_ref[top0,:]=zero

def parent_base(pos,everything,wc,par):
    vm=pl.BlockSpec(memory_space=pltpu.VMEM)
    cs,rows,_=wc.shape; slots=everything[0].shape[1]-PARENT_PIVOTS
    return pl.pallas_call(parent_kernel,
        out_shape=jax.ShapeDtypeStruct(par.shape,jnp.float32),
        in_specs=[pl.BlockSpec(memory_space=pltpu.SMEM)]+[vm]*(2+len(everything)),
        out_specs=vm,
        scratch_shapes=[pltpu.VMEM((BLK,BLK),jnp.float32),pltpu.VMEM((BLK,BLK),jnp.float32),
            pltpu.VMEM((slots,rows,BLK),jnp.float32),pltpu.VMEM((PARENT_PIVOTS,rows,BLK),jnp.float32)],
        compiler_params=pltpu.CompilerParams(vmem_limit_bytes=20<<20),
        name="parent_base")(pos,*everything,wc,par)

def extend_kernel(idx_ref, flag_ref, base_ref, recv_ref, out_ref):
    out_ref[...]=base_ref[...]
    groups,quota=recv_ref.shape[0],recv_ref.shape[1]
    cs=PARENT_CSLOTS
    @pl.when(flag_ref[0]>0)
    def _():
        for q in range(quota):
            for g in range(groups):
                start=idx_ref[q,g]
                at=pl.ds(start,BLK,stride=cs)
                out_ref[at,:]+=recv_ref[g,q]

def extend_add(idx,flag,base,recv):
    vm=pl.BlockSpec(memory_space=pltpu.VMEM); sm=pl.BlockSpec(memory_space=pltpu.SMEM)
    return pl.pallas_call(extend_kernel,
        out_shape=jax.ShapeDtypeStruct(base.shape,jnp.float32),
        in_specs=[sm,sm,vm,vm], out_specs=vm,
        input_output_aliases={2:0},
        compiler_params=pltpu.CompilerParams(vmem_limit_bytes=14<<20),
        name="extend_add")(idx,flag,base,recv)

def body(child_fronts, parent_front, child_map):
    XS,ZS=4,8
    leaf=lax.axis_index("leaf"); front=lax.axis_index("front")
    xpos=front//ZS; zpos=front%ZS
    own=child_fronts.reshape(child_fronts.shape[1],BLK)
    piv=CHILD_PIVOTS*BLK
    top=own[:piv]
    xg=[[x*ZS+z for x in range(XS)] for z in range(ZS)]
    zg=[[x*ZS+z for z in range(ZS)] for x in range(XS)]
    def spread(v,groups):
        copies=jnp.broadcast_to(v[None],(len(groups[0]),)+v.shape)
        return lax.all_to_all(copies,"front",split_axis=0,concat_axis=0,tiled=True,axis_index_groups=groups)
    leaves=lax.axis_size("leaf"); fronts=XS*ZS
    tie=lax.optimization_barrier
    def swap(v,axis,groups=None):
        return lax.all_to_all(v,axis,split_axis=0,concat_axis=0,tiled=True,axis_index_groups=groups)
    def copies(v,n):
        return jnp.broadcast_to(v[None],(n,)+v.shape)
    part=(CHILD_PIVOTS//2+1)*BLK
    piece=lax.dynamic_slice_in_dim(jnp.concatenate([top,top],0),zpos*BLK,part,0)
    def hop(d):
        return [(x*ZS+z,((x+d)%XS)*ZS+z) for x in range(XS) for z in range(ZS)]
    def rot(d):
        return [(x*ZS+z,x*ZS+(z+d)%ZS) for x in range(XS) for z in range(ZS)]
    def fperm(pairs,v):
        return lax.ppermute(v,"front",pairs)
    quarters=piece.reshape(XS,part//XS,BLK)
    piece=quarters[0]
    for d in range(1,XS):
        piece=jnp.where(xpos==d,fperm([(z,d*ZS+z) for z in range(ZS)],quarters[d]),piece)
    prow=parent_front.reshape(parent_front.shape[0],BLK*PARENT_CSLOTS,BLK)
    wc=swap(copies(prow[0],leaves),"leaf")[:PARENT_PIVOTS]
    piece,wc=tie((piece,wc))
    quarter=swap(copies(piece,ZS),"front",zg)
    wc=wc.reshape(PARENT_PIVOTS*BLK,PARENT_CSLOTS,BLK).transpose(1,0,2)
    quarter,top1,wc=tie((quarter,top,wc))
    q3=fperm(hop(1),quarter); q1=fperm(hop(-1),quarter)
    g7=fperm(rot(1),top1); g1=fperm(rot(-1),top1)
    got=swap(wc.reshape(PARENT_CSLOTS,fronts,8,BLK).transpose(1,0,2,3),"front")
    mine=lax.dynamic_index_in_dim(got.reshape(XS,ZS,PARENT_CSLOTS,8,BLK),leaf,axis=1,keepdims=False)
    mine=jnp.concatenate([mine.reshape(XS*PARENT_CSLOTS,8,BLK),got[:PARENT_PIVOTS,0]],0)
    q1,q3,g1,g7,top1,mine=tie((q1,q3,g1,g7,top1,mine))
    q2a=fperm(hop(1),q3[:ZS//2]); q2b=fperm(hop(-1),q1[ZS//2:])
    half=piv//2
    g6=fperm(rot(2),top1); g2=fperm(rot(-2),top1)
    every=swap(copies(mine,ZS),"front",zg)
    q2a,q2b,top2,every=tie((q2a,q2b,top1,every))
    g5=fperm(rot(3),jnp.concatenate([top2,g7[:half]],0)); g3=fperm(rot(-3),jnp.concatenate([top2,g1[half:]],0))
    rhs=spread(top2,xg)
    pos=jnp.stack([front,zpos,xpos]).astype(jnp.int32)
    y,col=child_factor(pos,[quarter,q1,q2a,q2b,q3])
    first,g2,g3,g5,g6,rhs=tie((y[:8,:BLK],g2,g3,g5,g6,rhs))
    p0,p1,p2,p3=child_update(pos,first,[top1,g1,g2,g3,g5,g6,g7],y,rhs)
    ra=fperm(hop(1),p2[:half]); rb=fperm(hop(-1),p2[half:])
    r1=fperm(hop(1),p1); r3=fperm(hop(-1),p3)
    ra,rb=tie((ra,rb))
    ra=fperm(hop(1),ra); rb=fperm(hop(-1),rb)
    out,sent=combine(pos,[p0,r1,ra,rb,r3],own,col)
    quota=(own.shape[0]-piv)//BLK//leaves
    recv=lax.all_to_all(sent,"leaf",split_axis=0,concat_axis=0,tiled=True)
    everything=[every]+[fperm(hop(-d),every) for d in range(1,XS)]
    base=parent_base(jnp.stack([front,leaf,xpos]).astype(jnp.int32),everything,wc,prow.reshape(-1,BLK))
    rowsel=(jnp.arange(leaves)==leaf)
    rmap=jnp.sum(jnp.where(rowsel[None,None,:],child_map.reshape(leaves,quota,leaves),0),axis=2)
    vblk=front-CHILD_PIVOTS
    csel=(jnp.arange(child_map.shape[1])==vblk)
    cmap=jnp.sum(jnp.where(csel[None,:],child_map,0),axis=1)
    idx=((rmap//leaves)*(BLK*PARENT_CSLOTS)+(cmap//32)[:,None]).T.astype(jnp.int32)
    flag=(front>=CHILD_PIVOTS).astype(jnp.int32).reshape(1)
    parent=extend_add(idx,flag,base,recv)
    return out.reshape(child_fronts.shape),parent.reshape(parent_front.shape)


def solution(mesh):
    return jax.shard_map(
        body,
        mesh=mesh,
        in_specs=(
            P("leaf", None, None, "front", None),
            P(None, "leaf", None, None, "front", None),
            P(),
        ),
        out_specs=(
            P("leaf", None, None, "front", None),
            P(None, "leaf", None, None, "front", None),
        ),
        check_vma=False,
    )
```

```python
import jax, jax.numpy as jnp
from jax import lax
from jax.experimental import pallas as pl
from jax.experimental.pallas import tpu as pltpu
from jax.sharding import PartitionSpec as P

BLK=128
CHILD_PIVOTS=8
PARENT_PIVOTS=2
PARENT_CSLOTS=2
NB=16
HI=lax.Precision.HIGHEST

def mm(a,b):
    return jnp.dot(a,b,precision=HI,preferred_element_type=jnp.float32)

def split(a):
    hi=a.astype(jnp.bfloat16)
    return hi,(a-hi.astype(jnp.float32)).astype(jnp.bfloat16)

def mm3(a,b):
    ah,al=split(a); bh,bl=split(b)
    dot=lambda x,y: jnp.dot(x,y,preferred_element_type=jnp.float32)
    return dot(ah,bh)+(dot(ah,bl)+dot(al,bh))

def factor_block(a, u_ref, m_ref, nb=None):
    nb = nb or NB
    n=BLK
    rows=lax.broadcasted_iota(jnp.int32,(n,n),0); cols=lax.broadcasted_iota(jnp.int32,(n,n),1)
    inv=jnp.where(rows==cols,1.0,0.0).astype(jnp.float32)
    sub=lax.broadcasted_iota(jnp.int32,(nb,n),0)
    lane=lax.broadcasted_iota(jnp.int32,(nb,n),1)
    for c0 in range(0,n,nb):
        r=a[c0:c0+nb,:]; y=inv[c0:c0+nb,:]
        bc=[jnp.broadcast_to(r[:,c0+t:c0+t+1],(nb,n)) for t in range(nb)]
        piv=jnp.ones((nb,n),jnp.float32)
        for t in range(nb):
            p=jnp.broadcast_to(bc[t][t:t+1,:],(nb,n))
            piv=jnp.where(sub==t,p,piv)
            if t==nb-1: break
            m=jnp.where(sub>t,bc[t]*(1.0/p),0.0)
            for q in range(t+1,nb):
                bc[q]=bc[q]-m*jnp.broadcast_to(bc[q][t:t+1,:],(nb,n))
            r=r-m*jnp.broadcast_to(r[t:t+1,:],(nb,n))
            y=y-m*jnp.broadcast_to(y[t:t+1,:],(nb,n))
        scale=lax.rsqrt(piv)
        u=jnp.where(lane>=sub+c0,r*scale,0.0); y=y*scale
        u_ref[c0:c0+nb,:]=u; m_ref[c0:c0+nb,:]=y
        if c0+nb<n:
            upd=mm(u.T,jnp.concatenate([u,y],1))
            a=a-upd[:,:n]; inv=inv-upd[:,n:]

def child_kernel(pos_ref, q0_ref, q1_ref, q2a_ref, q2b_ref, q3_ref, yt_ref, col_ref, ring_ref, a_ref, y_ref, u_ref, m_ref, sem_ref):
    front=pos_ref[0]; xpos=pos_ref[2]; nblk,prow,_=q0_ref.shape; n=BLK*nblk; half=nblk//2
    for d,first,ref in ((0,0,q0_ref),(1,0,q1_ref),(2,0,q2a_ref),(2,nblk//2,q2b_ref),(3,0,q3_ref)):
        at=pl.multiple_of(((xpos+d)%4)*prow,8)
        for k in range(ref.shape[0]):
            ring_ref[first+k,pl.ds(at,prow),:]=ref[k]
    for k in range(nblk):
        for i in range(half+1):
            r=(k+i)%nblk
            if r>k:
                if i<half: a_ref[k*BLK:(k+1)*BLK,r*BLK:(r+1)*BLK]=ring_ref[k,i*BLK:(i+1)*BLK,:].T
            else:
                a_ref[r*BLK:(r+1)*BLK,k*BLK:(k+1)*BLK]=ring_ref[k,i*BLK:(i+1)*BLK,:]
    y_ref[...]=jnp.zeros((n,n),jnp.float32)
    col_ref[...]=jnp.zeros((n,BLK),jnp.float32)
    def step(k,carry):
        for s in range(nblk):
            @pl.when(k==s)
            def _(s=s):
                m_ref[...]=a_ref[s*BLK:(s+1)*BLK,s*BLK:(s+1)*BLK]
        factor_block(m_ref[...],u_ref,m_ref)
        for s in range(nblk):
            @pl.when(k==s)
            def _(s=s):
                lo=s*BLK; hi=lo+BLK
                m=m_ref[...]
                parts=[]
                if s: parts.append(y_ref[lo:hi,:lo])
                if hi<n: parts.append(a_ref[lo:hi,hi:])
                full=mm(m,jnp.concatenate(parts,1))
                yk=jnp.concatenate([full[:,:lo],m],1) if s else m
                y_ref[lo:hi,:hi]=yk
                pltpu.make_async_copy(y_ref.at[lo:hi],yt_ref.at[lo:hi],sem_ref.at[s]).start()
                rest=full[:,lo:]
                if hi<n:
                    upd=mm(rest.T,jnp.concatenate([yk,rest],1))
                    y_ref[hi:,:hi]-=upd[:,:hi]
                    a_ref[hi:,hi:]-=upd[:,hi:n]
                @pl.when(front==s)
                def _():
                    col_ref[lo:hi,:]=u_ref[...].T
                    for j in range(s+1,nblk):
                        col_ref[j*BLK:(j+1)*BLK,:]=rest[:,(j-s-1)*BLK:(j-s)*BLK].T
        return carry
    lax.fori_loop(0,nblk,step,0)
    for s in range(nblk):
        pltpu.make_async_copy(y_ref.at[s*BLK:(s+1)*BLK],yt_ref.at[s*BLK:(s+1)*BLK],sem_ref.at[s]).wait()

def child_factor(pos,parts):
    nblk,prow,_=parts[0].shape; n=nblk*BLK; quarters=len(parts)-1
    vm=pl.BlockSpec(memory_space=pltpu.VMEM)
    return pl.pallas_call(child_kernel,
        out_shape=(pltpu.HBM((n,n),jnp.float32),jax.ShapeDtypeStruct((n,BLK),jnp.float32)),
        in_specs=[pl.BlockSpec(memory_space=pltpu.SMEM)]+[vm]*len(parts),
        out_specs=(pl.BlockSpec(memory_space=pltpu.HBM),vm),
        scratch_shapes=[pltpu.VMEM((nblk,quarters*prow,BLK),jnp.float32),pltpu.VMEM((n,n),jnp.float32),pltpu.VMEM((n,n),jnp.float32),pltpu.VMEM((BLK,BLK),jnp.float32),pltpu.VMEM((BLK,BLK),jnp.float32),pltpu.SemaphoreType.DMA((nblk,))],
        compiler_params=pltpu.CompilerParams(vmem_limit_bytes=30<<20),
        name="child_factor")(pos,*parts)


UPD=2

def update_kernel(pos_ref, *refs):
    far=refs[:9]; outs=refs[9:13]; near=refs[13:22]; zh_ref,zl_ref,sem_ref=refs[22:]
    fetch=[pltpu.make_async_copy(a.at[:,:b.shape[1]] if len(b.shape)==3 else a,b,sem_ref.at[i]) for i,(a,b) in enumerate(zip(far,near))]
    for i in (7,8,0,1,2,3,4,5,6): fetch[i].start()
    g=near[:7]; y_ref=near[7]; f_ref=near[8]
    n=y_ref.shape[0]
    zpos=pos_ref[1]; xpos=pos_ref[2]; planes=len(outs)
    dot=lambda x,y: jnp.dot(x,y,preferred_element_type=jnp.float32)
    fetch[7].wait()
    yh,yl=split(y_ref[...])
    fetch[8].wait()
    fh,fl=split(jnp.concatenate([f_ref[(xpos+d)%planes] for d in range(planes)],1))
    v=dot(yh,fh)+(dot(yh,fl)+dot(yl,fh))
    vh,vl=split(v.T)
    zt=dot(vh,yh)+(dot(vh,yl)+dot(vl,yh))
    zh,zl=split(zt)
    zh_ref[...]=zh; zl_ref[...]=zl
    zh,zl=split(y_ref[pl.ds(pl.multiple_of(zpos*BLK,BLK),BLK),:])
    for d in range(planes):
        @pl.when((xpos+d)%planes==0)
        def _(d=d):
            zh_ref[d*BLK:(d+1)*BLK]=zh; zl_ref[d*BLK:(d+1)*BLK]=zl
    for i in range(7): fetch[i].wait()
    blocks=[r[:n,:] for r in g]
    blocks.insert(4,jnp.concatenate([g[4][n:,:],g[3][n:,:]],0))
    for d in range(0,len(blocks),2):
        gh,gl=split(jnp.concatenate(blocks[d:d+2],1))
        prod=dot(zh_ref[...],gh)+(dot(zh_ref[...],gl)+dot(zl_ref[...],gh))
        for x in range(planes):
            for b in range(2):
                outs[x][(d+b)*BLK:(d+b+1)*BLK,:]=prod[x*BLK:(x+1)*BLK,b*BLK:(b+1)*BLK].T

def child_update(pos,gathered,y,rhs):
    piv=y.shape[0]; planes=rhs.shape[0]
    vm=pl.BlockSpec(memory_space=pltpu.VMEM); hbm=pl.BlockSpec(memory_space=pltpu.HBM)
    return pl.pallas_call(update_kernel,
        out_shape=(jax.ShapeDtypeStruct((piv,BLK),jnp.float32),)*planes,
        in_specs=[pl.BlockSpec(memory_space=pltpu.SMEM)]+[hbm]*(len(gathered)+2),
        out_specs=(vm,)*planes,
        scratch_shapes=[pltpu.VMEM(g.shape,jnp.float32) for g in gathered]+[pltpu.VMEM(y.shape,jnp.float32),pltpu.VMEM((planes,piv,BLK),jnp.float32),
            pltpu.VMEM((planes*BLK,piv),jnp.bfloat16),pltpu.VMEM((planes*BLK,piv),jnp.bfloat16),pltpu.SemaphoreType.DMA((len(gathered)+2,))],
        compiler_params=pltpu.CompilerParams(vmem_limit_bytes=44<<20),
        name="child_update")(pos,*[pltpu.with_memory_space_constraint(v,pltpu.HBM) for v in (*gathered,y,rhs)])

def combine_kernel(pos_ref, r0_ref, r1_ref, r2a_ref, r2b_ref, r3_ref, own_ref, col_ref, out_ref, sent_ref):
    zpos=pos_ref[1]; xpos=pos_ref[2]
    head=col_ref.shape[0]; nblk=r0_ref.shape[0]//BLK
    out_ref[:head,:]=col_ref[...]
    for d,first,ref in ((0,0,r0_ref),(1,0,r1_ref),(2,0,r2a_ref),(2,nblk//2,r2b_ref),(3,0,r3_ref)):
        src=(xpos-d+4)%4
        @pl.when(src>0)
        def _(first=first,ref=ref,src=src):
            for j in range(ref.shape[0]//BLK):
                blk=(zpos+first+j)%nblk
                at=pl.multiple_of(src*head+blk*BLK,BLK)
                r=ref[j*BLK:(j+1)*BLK,:]
                val=jnp.where(xpos==0,r,own_ref[pl.ds(at,BLK),:]-r)
                out_ref[pl.ds(at,BLK),:]=val
                sent_ref[blk,src-1]=val

def combine(pos,parts,own,col):
    vm=pl.BlockSpec(memory_space=pltpu.VMEM); nblk=parts[0].shape[0]//BLK
    return pl.pallas_call(combine_kernel,
        out_shape=(jax.ShapeDtypeStruct(own.shape,jnp.float32),jax.ShapeDtypeStruct((nblk,len(parts)-2,BLK,BLK),jnp.float32)),
        in_specs=[pl.BlockSpec(memory_space=pltpu.SMEM)]+[vm]*(2+len(parts)),
        out_specs=(vm,vm),
        compiler_params=pltpu.CompilerParams(vmem_limit_bytes=14<<20),
        name="combine")(pos,*parts,own,col)

def parent_kernel(pos_ref, e_ref, wc_ref, par_ref, out_ref, u_ref, m_ref, wr_ref, p11_ref):
    front=pos_ref[0]; leaf=pos_ref[1]
    slots=wr_ref.shape[0]; cs=wc_ref.shape[0]; xs=slots//cs
    for x in range(xs):
        for z in range(e_ref.shape[1]):
            first=8*(x*e_ref.shape[1]+z)
            for t in range(slots):
                wr_ref[(t%cs)*xs+t//cs,first:first+8,:]=e_ref[x,z,t]
            for p in range(PARENT_PIVOTS):
                p11_ref[p,first:first+8,:]=e_ref[x,z,slots+p]
    a0=p11_ref[0]; a1=p11_ref[1]
    factor_block(a0[:BLK],u_ref,m_ref)
    m0=m_ref[...]; u00=u_ref[...]
    u01=mm(m0,a1[:BLK])
    u_ref[...]=a1[BLK:]-mm(u01.T,u01)
    factor_block(u_ref[...],u_ref,m_ref)
    m1=m_ref[...]; u11=u_ref[...]
    w=jnp.concatenate([wc_ref[c] for c in range(cs)]+[wr_ref[s] for s in range(slots)],1)
    v0=mm(m0,w[:BLK])
    v1=mm(m1,w[BLK:]-mm(u01.T,v0))
    v=jnp.concatenate([v0,v1],0)
    lrows=v[:,cs*BLK:].T
    prod=mm(lrows,v[:,:cs*BLK])
    for s in range(slots):
        for c in range(cs):
            at=pl.ds(s*BLK*cs+c,BLK,stride=cs)
            out_ref[at,:]=par_ref[at,:]-prod[s*BLK:(s+1)*BLK,c*BLK:(c+1)*BLK]
    for p in range(PARENT_PIVOTS):
        @pl.when(front==p)
        def _(p=p):
            for s in range(slots):
                out_ref[pl.ds(s*BLK*cs,BLK,stride=cs),:]=lrows[s*BLK:(s+1)*BLK,p*BLK:(p+1)*BLK]
    top0=pl.ds(0,BLK,stride=cs)
    zero=jnp.zeros((BLK,BLK),jnp.float32)
    @pl.when(leaf<PARENT_PIVOTS)
    def _():
        for c in range(1,cs):
            out_ref[pl.ds(c,BLK,stride=cs),:]=zero
        @pl.when(front>=PARENT_PIVOTS)
        def _():
            out_ref[top0,:]=zero
        @pl.when((front==0)&(leaf==0))
        def _():
            out_ref[top0,:]=u00.T
        @pl.when((front==1)&(leaf==1))
        def _():
            out_ref[top0,:]=u11.T
        @pl.when((front==1)&(leaf==0))
        def _():
            out_ref[top0,:]=zero

def parent_base(pos,everything,wc,par):
    vm=pl.BlockSpec(memory_space=pltpu.VMEM)
    cs,rows,_=wc.shape; slots=everything.shape[2]-PARENT_PIVOTS
    return pl.pallas_call(parent_kernel,
        out_shape=jax.ShapeDtypeStruct(par.shape,jnp.float32),
        in_specs=[pl.BlockSpec(memory_space=pltpu.SMEM)]+[vm]*3,
        out_specs=vm,
        scratch_shapes=[pltpu.VMEM((BLK,BLK),jnp.float32),pltpu.VMEM((BLK,BLK),jnp.float32),
            pltpu.VMEM((slots,rows,BLK),jnp.float32),pltpu.VMEM((PARENT_PIVOTS,rows,BLK),jnp.float32)],
        compiler_params=pltpu.CompilerParams(vmem_limit_bytes=20<<20),
        name="parent_base")(pos,everything,wc,par)

def extend_kernel(idx_ref, flag_ref, base_ref, recv_ref, out_ref):
    out_ref[...]=base_ref[...]
    groups,quota=recv_ref.shape[0],recv_ref.shape[1]
    cs=PARENT_CSLOTS
    @pl.when(flag_ref[0]>0)
    def _():
        for q in range(quota):
            for g in range(groups):
                start=idx_ref[q,g]
                at=pl.ds(start,BLK,stride=cs)
                out_ref[at,:]+=recv_ref[g,q]

def extend_add(idx,flag,base,recv):
    vm=pl.BlockSpec(memory_space=pltpu.VMEM); sm=pl.BlockSpec(memory_space=pltpu.SMEM)
    return pl.pallas_call(extend_kernel,
        out_shape=jax.ShapeDtypeStruct(base.shape,jnp.float32),
        in_specs=[sm,sm,vm,vm], out_specs=vm,
        input_output_aliases={2:0},
        compiler_params=pltpu.CompilerParams(vmem_limit_bytes=14<<20),
        name="extend_add")(idx,flag,base,recv)

def body(child_fronts, parent_front, child_map):
    XS,ZS=4,8
    leaf=lax.axis_index("leaf"); front=lax.axis_index("front")
    xpos=front//ZS; zpos=front%ZS
    own=child_fronts.reshape(child_fronts.shape[1],BLK)
    piv=CHILD_PIVOTS*BLK
    top=own[:piv]
    xg=[[x*ZS+z for x in range(XS)] for z in range(ZS)]
    zg=[[x*ZS+z for z in range(ZS)] for x in range(XS)]
    def spread(v,groups):
        copies=jnp.broadcast_to(v[None],(len(groups[0]),)+v.shape)
        return lax.all_to_all(copies,"front",split_axis=0,concat_axis=0,tiled=True,axis_index_groups=groups)
    leaves=lax.axis_size("leaf"); fronts=XS*ZS
    tie=lax.optimization_barrier
    def swap(v,axis,groups=None):
        return lax.all_to_all(v,axis,split_axis=0,concat_axis=0,tiled=True,axis_index_groups=groups)
    def copies(v,n):
        return jnp.broadcast_to(v[None],(n,)+v.shape)
    part=(CHILD_PIVOTS//2+1)*BLK
    piece=lax.dynamic_slice_in_dim(jnp.concatenate([top,top],0),zpos*BLK,part,0)
    def hop(d):
        return [(x*ZS+z,((x+d)%XS)*ZS+z) for x in range(XS) for z in range(ZS)]
    def rot(d):
        return [(x*ZS+z,x*ZS+(z+d)%ZS) for x in range(XS) for z in range(ZS)]
    def fperm(pairs,v):
        return lax.ppermute(v,"front",pairs)
    quarters=piece.reshape(XS,part//XS,BLK)
    piece=quarters[0]
    for d in range(1,XS):
        piece=jnp.where(xpos==d,fperm([(z,d*ZS+z) for z in range(ZS)],quarters[d]),piece)
    prow=parent_front.reshape(parent_front.shape[0],BLK*PARENT_CSLOTS,BLK)
    wc=swap(copies(prow[0],leaves),"leaf")[:PARENT_PIVOTS]
    piece,wc=tie((piece,wc))
    quarter=swap(copies(piece,ZS),"front",zg)
    wc=wc.reshape(PARENT_PIVOTS*BLK,PARENT_CSLOTS,BLK).transpose(1,0,2)
    quarter,top1,wc=tie((quarter,top,wc))
    q3=fperm(hop(1),quarter); q1=fperm(hop(-1),quarter)
    g7=fperm(rot(1),top1); g1=fperm(rot(-1),top1)
    got=swap(wc.reshape(PARENT_CSLOTS,fronts,8,BLK).transpose(1,0,2,3),"front")
    mine=lax.dynamic_index_in_dim(got.reshape(XS,ZS,PARENT_CSLOTS,8,BLK),leaf,axis=1,keepdims=False)
    mine=jnp.concatenate([mine.reshape(XS*PARENT_CSLOTS,8,BLK),got[:PARENT_PIVOTS,0]],0)
    q1,q3,g1,g7,top1,mine=tie((q1,q3,g1,g7,top1,mine))
    q2a=fperm(hop(1),q3[:ZS//2]); q2b=fperm(hop(-1),q1[ZS//2:])
    half=piv//2
    g6=fperm(rot(2),top1); g2=fperm(rot(-2),top1)
    every=swap(copies(mine,ZS),"front",zg)
    q2a,q2b,top2,every=tie((q2a,q2b,top1,every))
    g5=fperm(rot(3),jnp.concatenate([top2,g7[:half]],0)); g3=fperm(rot(-3),jnp.concatenate([top2,g1[half:]],0))
    rhs=spread(jnp.concatenate([top2,every.reshape(-1,BLK)],0),xg)
    pos=jnp.stack([front,zpos,xpos]).astype(jnp.int32)
    y,col=child_factor(pos,[quarter,q1,q2a,q2b,q3])
    y,g2,g3,g5,g6,rhs=tie((y,g2,g3,g5,g6,rhs))
    p0,p1,p2,p3=child_update(pos,[top1,g1,g2,g3,g5,g6,g7],y,rhs)
    ra=fperm(hop(1),p2[:half]); rb=fperm(hop(-1),p2[half:])
    r1=fperm(hop(1),p1); r3=fperm(hop(-1),p3)
    ra,rb=tie((ra,rb))
    ra=fperm(hop(1),ra); rb=fperm(hop(-1),rb)
    out,sent=combine(pos,[p0,r1,ra,rb,r3],own,col)
    quota=(own.shape[0]-piv)//BLK//leaves
    recv=lax.all_to_all(sent,"leaf",split_axis=0,concat_axis=0,tiled=True)
    everything=rhs[:,piv:].reshape(XS,ZS,-1,8,BLK)
    base=parent_base(jnp.stack([front,leaf]).astype(jnp.int32),everything,wc,prow.reshape(-1,BLK))
    rowsel=(jnp.arange(leaves)==leaf)
    rmap=jnp.sum(jnp.where(rowsel[None,None,:],child_map.reshape(leaves,quota,leaves),0),axis=2)
    vblk=front-CHILD_PIVOTS
    csel=(jnp.arange(child_map.shape[1])==vblk)
    cmap=jnp.sum(jnp.where(csel[None,:],child_map,0),axis=1)
    idx=((rmap//leaves)*(BLK*PARENT_CSLOTS)+(cmap//32)[:,None]).T.astype(jnp.int32)
    flag=(front>=CHILD_PIVOTS).astype(jnp.int32).reshape(1)
    parent=extend_add(idx,flag,base,recv)
    return out.reshape(child_fronts.shape),parent.reshape(parent_front.shape)


def solution(mesh):
    return jax.shard_map(
        body,
        mesh=mesh,
        in_specs=(
            P("leaf", None, None, "front", None),
            P(None, "leaf", None, None, "front", None),
            P(),
        ),
        out_specs=(
            P("leaf", None, None, "front", None),
            P(None, "leaf", None, None, "front", None),
        ),
        check_vma=False,
    )
```

```python
import jax, jax.numpy as jnp
from jax import lax
from jax.experimental import pallas as pl
from jax.experimental.pallas import tpu as pltpu
from jax.sharding import PartitionSpec as P

BLK=128
CHILD_PIVOTS=8
PARENT_PIVOTS=2
PARENT_CSLOTS=2
NB=32
HI=lax.Precision.HIGHEST

def mm(a,b):
    return jnp.dot(a,b,precision=HI,preferred_element_type=jnp.float32)

def split(a):
    hi=a.astype(jnp.bfloat16)
    return hi,(a-hi.astype(jnp.float32)).astype(jnp.bfloat16)

def mm3(a,b):
    ah,al=split(a); bh,bl=split(b)
    dot=lambda x,y: jnp.dot(x,y,preferred_element_type=jnp.float32)
    return dot(ah,bh)+(dot(ah,bl)+dot(al,bh))

def factor_block(a, u_ref, m_ref, mul, nb=None):
    nb = nb or NB
    n=BLK
    rows=lax.broadcasted_iota(jnp.int32,(n,n),0); cols=lax.broadcasted_iota(jnp.int32,(n,n),1)
    inv=jnp.where(rows==cols,1.0,0.0).astype(jnp.float32)
    sub=lax.broadcasted_iota(jnp.int32,(nb,n),0)
    lane=lax.broadcasted_iota(jnp.int32,(nb,n),1)
    for c0 in range(0,n,nb):
        r=a[c0:c0+nb,:]; y=inv[c0:c0+nb,:]
        bc=[jnp.broadcast_to(r[:,c0+t:c0+t+1],(nb,n)) for t in range(nb)]
        piv=jnp.ones((nb,n),jnp.float32)
        for t in range(nb):
            p=jnp.broadcast_to(bc[t][t:t+1,:],(nb,n))
            piv=jnp.where(sub==t,p,piv)
            if t==nb-1: break
            m=jnp.where(sub>t,bc[t]*(1.0/p),0.0)
            for q in range(t+1,nb):
                bc[q]=bc[q]-m*jnp.broadcast_to(bc[q][t:t+1,:],(nb,n))
            r=r-m*jnp.broadcast_to(r[t:t+1,:],(nb,n))
            y=y-m*jnp.broadcast_to(y[t:t+1,:],(nb,n))
        scale=lax.rsqrt(piv)
        u=jnp.where(lane>=sub+c0,r*scale,0.0); y=y*scale
        u_ref[c0:c0+nb,:]=u; m_ref[c0:c0+nb,:]=y
        if c0+nb<n:
            upd=mul(u.T,jnp.concatenate([u,y],1))
            a=a-upd[:,:n]; inv=inv-upd[:,n:]

def child_kernel(pos_ref, q0_ref, q1_ref, q2a_ref, q2b_ref, q3_ref, yt_ref, col_ref, ring_ref, a_ref, y_ref, u_ref, m_ref, sem_ref):
    front=pos_ref[0]; xpos=pos_ref[2]; nblk,prow,_=q0_ref.shape; n=BLK*nblk; half=nblk//2
    for d,first,ref in ((0,0,q0_ref),(1,0,q1_ref),(2,0,q2a_ref),(2,nblk//2,q2b_ref),(3,0,q3_ref)):
        at=pl.multiple_of(((xpos+d)%4)*prow,8)
        for k in range(ref.shape[0]):
            ring_ref[first+k,pl.ds(at,prow),:]=ref[k]
    for k in range(nblk):
        for i in range(half+1):
            r=(k+i)%nblk
            if r>k:
                if i<half: a_ref[k*BLK:(k+1)*BLK,r*BLK:(r+1)*BLK]=ring_ref[k,i*BLK:(i+1)*BLK,:].T
            else:
                a_ref[r*BLK:(r+1)*BLK,k*BLK:(k+1)*BLK]=ring_ref[k,i*BLK:(i+1)*BLK,:]
    y_ref[...]=jnp.zeros((n,n),jnp.float32)
    col_ref[...]=jnp.zeros((n,BLK),jnp.float32)
    def step(k,carry):
        for s in range(nblk):
            @pl.when(k==s)
            def _(s=s):
                m_ref[...]=a_ref[s*BLK:(s+1)*BLK,s*BLK:(s+1)*BLK]
        factor_block(m_ref[...],u_ref,m_ref,mm3)
        for s in range(nblk):
            @pl.when(k==s)
            def _(s=s):
                lo=s*BLK; hi=lo+BLK
                m=m_ref[...]
                parts=[]
                if s: parts.append(y_ref[lo:hi,:lo])
                if hi<n: parts.append(a_ref[lo:hi,hi:])
                full=mm3(m,jnp.concatenate(parts,1))
                yk=jnp.concatenate([full[:,:lo],m],1) if s else m
                y_ref[lo:hi,:hi]=yk
                pltpu.make_async_copy(y_ref.at[lo:hi],yt_ref.at[lo:hi],sem_ref.at[s]).start()
                rest=full[:,lo:]
                if hi<n:
                    upd=mm3(rest.T,jnp.concatenate([yk,rest],1))
                    y_ref[hi:,:hi]-=upd[:,:hi]
                    a_ref[hi:,hi:]-=upd[:,hi:n]
                @pl.when(front==s)
                def _():
                    col_ref[lo:hi,:]=u_ref[...].T
                    for j in range(s+1,nblk):
                        col_ref[j*BLK:(j+1)*BLK,:]=rest[:,(j-s-1)*BLK:(j-s)*BLK].T
        return carry
    lax.fori_loop(0,nblk,step,0)
    for s in range(nblk):
        pltpu.make_async_copy(y_ref.at[s*BLK:(s+1)*BLK],yt_ref.at[s*BLK:(s+1)*BLK],sem_ref.at[s]).wait()

def child_factor(pos,parts):
    nblk,prow,_=parts[0].shape; n=nblk*BLK; quarters=len(parts)-1
    vm=pl.BlockSpec(memory_space=pltpu.VMEM)
    return pl.pallas_call(child_kernel,
        out_shape=(pltpu.HBM((n,n),jnp.float32),jax.ShapeDtypeStruct((n,BLK),jnp.float32)),
        in_specs=[pl.BlockSpec(memory_space=pltpu.SMEM)]+[vm]*len(parts),
        out_specs=(pl.BlockSpec(memory_space=pltpu.HBM),vm),
        scratch_shapes=[pltpu.VMEM((nblk,quarters*prow,BLK),jnp.float32),pltpu.VMEM((n,n),jnp.float32),pltpu.VMEM((n,n),jnp.float32),pltpu.VMEM((BLK,BLK),jnp.float32),pltpu.VMEM((BLK,BLK),jnp.float32),pltpu.SemaphoreType.DMA((nblk,))],
        compiler_params=pltpu.CompilerParams(vmem_limit_bytes=30<<20),
        name="child_factor")(pos,*parts)


UPD=2

def update_kernel(pos_ref, *refs):
    far=refs[:9]; outs=refs[9:13]; near=refs[13:22]; zh_ref,zl_ref,sem_ref=refs[22:]
    fetch=[pltpu.make_async_copy(a.at[:,:b.shape[1]] if len(b.shape)==3 else a,b,sem_ref.at[i]) for i,(a,b) in enumerate(zip(far,near))]
    for i in (7,8,0,1,2,3,4,5,6): fetch[i].start()
    g=near[:7]; y_ref=near[7]; f_ref=near[8]
    n=y_ref.shape[0]
    zpos=pos_ref[1]; xpos=pos_ref[2]; planes=len(outs)
    dot=lambda x,y: jnp.dot(x,y,preferred_element_type=jnp.float32)
    fetch[7].wait()
    yh,yl=split(y_ref[...])
    fetch[8].wait()
    fh,fl=split(jnp.concatenate([f_ref[(xpos+d)%planes] for d in range(planes)],1))
    v=dot(yh,fh)+(dot(yh,fl)+dot(yl,fh))
    vh,vl=split(v.T)
    zt=dot(vh,yh)+(dot(vh,yl)+dot(vl,yh))
    zh,zl=split(zt)
    zh_ref[...]=zh; zl_ref[...]=zl
    zh,zl=split(y_ref[pl.ds(pl.multiple_of(zpos*BLK,BLK),BLK),:])
    for d in range(planes):
        @pl.when((xpos+d)%planes==0)
        def _(d=d):
            zh_ref[d*BLK:(d+1)*BLK]=zh; zl_ref[d*BLK:(d+1)*BLK]=zl
    for i in range(7): fetch[i].wait()
    blocks=[r[:n,:] for r in g]
    blocks.insert(4,jnp.concatenate([g[4][n:,:],g[3][n:,:]],0))
    for d in range(0,len(blocks),2):
        gh,gl=split(jnp.concatenate(blocks[d:d+2],1))
        prod=dot(zh_ref[...],gh)+(dot(zh_ref[...],gl)+dot(zl_ref[...],gh))
        for x in range(planes):
            for b in range(2):
                outs[x][(d+b)*BLK:(d+b+1)*BLK,:]=prod[x*BLK:(x+1)*BLK,b*BLK:(b+1)*BLK].T

def child_update(pos,gathered,y,rhs):
    piv=y.shape[0]; planes=rhs.shape[0]
    vm=pl.BlockSpec(memory_space=pltpu.VMEM); hbm=pl.BlockSpec(memory_space=pltpu.HBM)
    return pl.pallas_call(update_kernel,
        out_shape=(jax.ShapeDtypeStruct((piv,BLK),jnp.float32),)*planes,
        in_specs=[pl.BlockSpec(memory_space=pltpu.SMEM)]+[hbm]*(len(gathered)+2),
        out_specs=(vm,)*planes,
        scratch_shapes=[pltpu.VMEM(g.shape,jnp.float32) for g in gathered]+[pltpu.VMEM(y.shape,jnp.float32),pltpu.VMEM((planes,piv,BLK),jnp.float32),
            pltpu.VMEM((planes*BLK,piv),jnp.bfloat16),pltpu.VMEM((planes*BLK,piv),jnp.bfloat16),pltpu.SemaphoreType.DMA((len(gathered)+2,))],
        compiler_params=pltpu.CompilerParams(vmem_limit_bytes=44<<20),
        name="child_update")(pos,*[pltpu.with_memory_space_constraint(v,pltpu.HBM) for v in (*gathered,y,rhs)])

def combine_kernel(pos_ref, r0_ref, r1_ref, r2a_ref, r2b_ref, r3_ref, own_ref, col_ref, out_ref, sent_ref):
    zpos=pos_ref[1]; xpos=pos_ref[2]
    head=col_ref.shape[0]; nblk=r0_ref.shape[0]//BLK
    out_ref[:head,:]=col_ref[...]
    for d,first,ref in ((0,0,r0_ref),(1,0,r1_ref),(2,0,r2a_ref),(2,nblk//2,r2b_ref),(3,0,r3_ref)):
        src=(xpos-d+4)%4
        @pl.when(src>0)
        def _(first=first,ref=ref,src=src):
            for j in range(ref.shape[0]//BLK):
                blk=(zpos+first+j)%nblk
                at=pl.multiple_of(src*head+blk*BLK,BLK)
                r=ref[j*BLK:(j+1)*BLK,:]
                val=jnp.where(xpos==0,r,own_ref[pl.ds(at,BLK),:]-r)
                out_ref[pl.ds(at,BLK),:]=val
                sent_ref[blk,src-1]=val

def combine(pos,parts,own,col):
    vm=pl.BlockSpec(memory_space=pltpu.VMEM); nblk=parts[0].shape[0]//BLK
    return pl.pallas_call(combine_kernel,
        out_shape=(jax.ShapeDtypeStruct(own.shape,jnp.float32),jax.ShapeDtypeStruct((nblk,len(parts)-2,BLK,BLK),jnp.float32)),
        in_specs=[pl.BlockSpec(memory_space=pltpu.SMEM)]+[vm]*(2+len(parts)),
        out_specs=(vm,vm),
        compiler_params=pltpu.CompilerParams(vmem_limit_bytes=14<<20),
        name="combine")(pos,*parts,own,col)

def parent_kernel(pos_ref, e_ref, wc_ref, par_ref, out_ref, u_ref, m_ref, wr_ref, p11_ref):
    front=pos_ref[0]; leaf=pos_ref[1]
    slots=wr_ref.shape[0]; cs=wc_ref.shape[0]; xs=slots//cs
    for x in range(xs):
        for z in range(e_ref.shape[1]):
            first=8*(x*e_ref.shape[1]+z)
            for t in range(slots):
                wr_ref[(t%cs)*xs+t//cs,first:first+8,:]=e_ref[x,z,t]
            for p in range(PARENT_PIVOTS):
                p11_ref[p,first:first+8,:]=e_ref[x,z,slots+p]
    a0=p11_ref[0]; a1=p11_ref[1]
    factor_block(a0[:BLK],u_ref,m_ref,mm)
    m0=m_ref[...]; u00=u_ref[...]
    u01=mm(m0,a1[:BLK])
    u_ref[...]=a1[BLK:]-mm(u01.T,u01)
    factor_block(u_ref[...],u_ref,m_ref,mm)
    m1=m_ref[...]; u11=u_ref[...]
    w=jnp.concatenate([wc_ref[c] for c in range(cs)]+[wr_ref[s] for s in range(slots)],1)
    v0=mm(m0,w[:BLK])
    v1=mm(m1,w[BLK:]-mm(u01.T,v0))
    v=jnp.concatenate([v0,v1],0)
    lrows=v[:,cs*BLK:].T
    prod=mm(lrows,v[:,:cs*BLK])
    for s in range(slots):
        for c in range(cs):
            at=pl.ds(s*BLK*cs+c,BLK,stride=cs)
            out_ref[at,:]=par_ref[at,:]-prod[s*BLK:(s+1)*BLK,c*BLK:(c+1)*BLK]
    for p in range(PARENT_PIVOTS):
        @pl.when(front==p)
        def _(p=p):
            for s in range(slots):
                out_ref[pl.ds(s*BLK*cs,BLK,stride=cs),:]=lrows[s*BLK:(s+1)*BLK,p*BLK:(p+1)*BLK]
    top0=pl.ds(0,BLK,stride=cs)
    zero=jnp.zeros((BLK,BLK),jnp.float32)
    @pl.when(leaf<PARENT_PIVOTS)
    def _():
        for c in range(1,cs):
            out_ref[pl.ds(c,BLK,stride=cs),:]=zero
        @pl.when(front>=PARENT_PIVOTS)
        def _():
            out_ref[top0,:]=zero
        @pl.when((front==0)&(leaf==0))
        def _():
            out_ref[top0,:]=u00.T
        @pl.when((front==1)&(leaf==1))
        def _():
            out_ref[top0,:]=u11.T
        @pl.when((front==1)&(leaf==0))
        def _():
            out_ref[top0,:]=zero

def parent_base(pos,everything,wc,par):
    vm=pl.BlockSpec(memory_space=pltpu.VMEM)
    cs,rows,_=wc.shape; slots=everything.shape[2]-PARENT_PIVOTS
    return pl.pallas_call(parent_kernel,
        out_shape=jax.ShapeDtypeStruct(par.shape,jnp.float32),
        in_specs=[pl.BlockSpec(memory_space=pltpu.SMEM)]+[vm]*3,
        out_specs=vm,
        scratch_shapes=[pltpu.VMEM((BLK,BLK),jnp.float32),pltpu.VMEM((BLK,BLK),jnp.float32),
            pltpu.VMEM((slots,rows,BLK),jnp.float32),pltpu.VMEM((PARENT_PIVOTS,rows,BLK),jnp.float32)],
        compiler_params=pltpu.CompilerParams(vmem_limit_bytes=20<<20),
        name="parent_base")(pos,everything,wc,par)

def extend_kernel(idx_ref, flag_ref, base_ref, recv_ref, out_ref):
    out_ref[...]=base_ref[...]
    groups,quota=recv_ref.shape[0],recv_ref.shape[1]
    cs=PARENT_CSLOTS
    @pl.when(flag_ref[0]>0)
    def _():
        for q in range(quota):
            for g in range(groups):
                start=idx_ref[q,g]
                at=pl.ds(start,BLK,stride=cs)
                out_ref[at,:]+=recv_ref[g,q]

def extend_add(idx,flag,base,recv):
    vm=pl.BlockSpec(memory_space=pltpu.VMEM); sm=pl.BlockSpec(memory_space=pltpu.SMEM)
    return pl.pallas_call(extend_kernel,
        out_shape=jax.ShapeDtypeStruct(base.shape,jnp.float32),
        in_specs=[sm,sm,vm,vm], out_specs=vm,
        input_output_aliases={2:0},
        compiler_params=pltpu.CompilerParams(vmem_limit_bytes=14<<20),
        name="extend_add")(idx,flag,base,recv)

def body(child_fronts, parent_front, child_map):
    XS,ZS=4,8
    leaf=lax.axis_index("leaf"); front=lax.axis_index("front")
    xpos=front//ZS; zpos=front%ZS
    own=child_fronts.reshape(child_fronts.shape[1],BLK)
    piv=CHILD_PIVOTS*BLK
    top=own[:piv]
    xg=[[x*ZS+z for x in range(XS)] for z in range(ZS)]
    zg=[[x*ZS+z for z in range(ZS)] for x in range(XS)]
    def spread(v,groups):
        copies=jnp.broadcast_to(v[None],(len(groups[0]),)+v.shape)
        return lax.all_to_all(copies,"front",split_axis=0,concat_axis=0,tiled=True,axis_index_groups=groups)
    leaves=lax.axis_size("leaf"); fronts=XS*ZS
    tie=lax.optimization_barrier
    def swap(v,axis,groups=None):
        return lax.all_to_all(v,axis,split_axis=0,concat_axis=0,tiled=True,axis_index_groups=groups)
    def copies(v,n):
        return jnp.broadcast_to(v[None],(n,)+v.shape)
    part=(CHILD_PIVOTS//2+1)*BLK
    piece=lax.dynamic_slice_in_dim(jnp.concatenate([top,top],0),zpos*BLK,part,0)
    def hop(d):
        return [(x*ZS+z,((x+d)%XS)*ZS+z) for x in range(XS) for z in range(ZS)]
    def rot(d):
        return [(x*ZS+z,x*ZS+(z+d)%ZS) for x in range(XS) for z in range(ZS)]
    def fperm(pairs,v):
        return lax.ppermute(v,"front",pairs)
    quarters=piece.reshape(XS,part//XS,BLK)
    piece=quarters[0]
    for d in range(1,XS):
        piece=jnp.where(xpos==d,fperm([(z,d*ZS+z) for z in range(ZS)],quarters[d]),piece)
    prow=parent_front.reshape(parent_front.shape[0],BLK*PARENT_CSLOTS,BLK)
    wc=swap(copies(prow[0],leaves),"leaf")[:PARENT_PIVOTS]
    piece,wc=tie((piece,wc))
    quarter=swap(copies(piece,ZS),"front",zg)
    wc=wc.reshape(PARENT_PIVOTS*BLK,PARENT_CSLOTS,BLK).transpose(1,0,2)
    quarter,top1,wc=tie((quarter,top,wc))
    q3=fperm(hop(1),quarter); q1=fperm(hop(-1),quarter)
    g7=fperm(rot(1),top1); g1=fperm(rot(-1),top1)
    got=swap(wc.reshape(PARENT_CSLOTS,fronts,8,BLK).transpose(1,0,2,3),"front")
    mine=lax.dynamic_index_in_dim(got.reshape(XS,ZS,PARENT_CSLOTS,8,BLK),leaf,axis=1,keepdims=False)
    mine=jnp.concatenate([mine.reshape(XS*PARENT_CSLOTS,8,BLK),got[:PARENT_PIVOTS,0]],0)
    q1,q3,g1,g7,top1,mine=tie((q1,q3,g1,g7,top1,mine))
    q2a=fperm(hop(1),q3[:ZS//2]); q2b=fperm(hop(-1),q1[ZS//2:])
    half=piv//2
    g6=fperm(rot(2),top1); g2=fperm(rot(-2),top1)
    every=swap(copies(mine,ZS),"front",zg)
    q2a,q2b,top2,every=tie((q2a,q2b,top1,every))
    g5=fperm(rot(3),jnp.concatenate([top2,g7[:half]],0)); g3=fperm(rot(-3),jnp.concatenate([top2,g1[half:]],0))
    rhs=spread(jnp.concatenate([top2,every.reshape(-1,BLK)],0),xg)
    pos=jnp.stack([front,zpos,xpos]).astype(jnp.int32)
    y,col=child_factor(pos,[quarter,q1,q2a,q2b,q3])
    y,g2,g3,g5,g6,rhs=tie((y,g2,g3,g5,g6,rhs))
    p0,p1,p2,p3=child_update(pos,[top1,g1,g2,g3,g5,g6,g7],y,rhs)
    ra=fperm(hop(1),p2[:half]); rb=fperm(hop(-1),p2[half:])
    r1=fperm(hop(1),p1); r3=fperm(hop(-1),p3)
    ra,rb=tie((ra,rb))
    ra=fperm(hop(1),ra); rb=fperm(hop(-1),rb)
    out,sent=combine(pos,[p0,r1,ra,rb,r3],own,col)
    quota=(own.shape[0]-piv)//BLK//leaves
    recv=lax.all_to_all(sent,"leaf",split_axis=0,concat_axis=0,tiled=True)
    everything=rhs[:,piv:].reshape(XS,ZS,-1,8,BLK)
    base=parent_base(jnp.stack([front,leaf]).astype(jnp.int32),everything,wc,prow.reshape(-1,BLK))
    rowsel=(jnp.arange(leaves)==leaf)
    rmap=jnp.sum(jnp.where(rowsel[None,None,:],child_map.reshape(leaves,quota,leaves),0),axis=2)
    vblk=front-CHILD_PIVOTS
    csel=(jnp.arange(child_map.shape[1])==vblk)
    cmap=jnp.sum(jnp.where(csel[None,:],child_map,0),axis=1)
    idx=((rmap//leaves)*(BLK*PARENT_CSLOTS)+(cmap//32)[:,None]).T.astype(jnp.int32)
    flag=(front>=CHILD_PIVOTS).astype(jnp.int32).reshape(1)
    parent=extend_add(idx,flag,base,recv)
    return out.reshape(child_fronts.shape),parent.reshape(parent_front.shape)


def solution(mesh):
    return jax.shard_map(
        body,
        mesh=mesh,
        in_specs=(
            P("leaf", None, None, "front", None),
            P(None, "leaf", None, None, "front", None),
            P(),
        ),
        out_specs=(
            P("leaf", None, None, "front", None),
            P(None, "leaf", None, None, "front", None),
        ),
        check_vma=False,
    )
```

```python
import jax, jax.numpy as jnp
from jax import lax
from jax.experimental import pallas as pl
from jax.experimental.pallas import tpu as pltpu
from jax.sharding import PartitionSpec as P

BLK=128
CHILD_PIVOTS=8
PARENT_PIVOTS=2
PARENT_CSLOTS=2
NB=32
HI=lax.Precision.HIGHEST

def mm(a,b):
    return jnp.dot(a,b,precision=HI,preferred_element_type=jnp.float32)

def split(a):
    hi=a.astype(jnp.bfloat16)
    return hi,(a-hi.astype(jnp.float32)).astype(jnp.bfloat16)

def mm3(a,b):
    ah,al=split(a); bh,bl=split(b)
    dot=lambda x,y: jnp.dot(x,y,preferred_element_type=jnp.float32)
    return dot(ah,bh)+(dot(ah,bl)+dot(al,bh))

def factor_block(a, u_ref, m_ref, mul, nb=None):
    nb = nb or NB
    n=BLK
    rows=lax.broadcasted_iota(jnp.int32,(n,n),0); cols=lax.broadcasted_iota(jnp.int32,(n,n),1)
    inv=jnp.where(rows==cols,1.0,0.0).astype(jnp.float32)
    sub=lax.broadcasted_iota(jnp.int32,(nb,n),0)
    lane=lax.broadcasted_iota(jnp.int32,(nb,n),1)
    for c0 in range(0,n,nb):
        r=a[c0:c0+nb,:]; y=inv[c0:c0+nb,:]
        bc=[jnp.broadcast_to(r[:,c0+t:c0+t+1],(nb,n)) for t in range(nb)]
        piv=jnp.ones((nb,n),jnp.float32)
        for t in range(nb):
            p=jnp.broadcast_to(bc[t][t:t+1,:],(nb,n))
            piv=jnp.where(sub==t,p,piv)
            if t==nb-1: break
            m=jnp.where(sub>t,bc[t]*(1.0/p),0.0)
            for q in range(t+1,nb):
                bc[q]=bc[q]-m*jnp.broadcast_to(bc[q][t:t+1,:],(nb,n))
            r=r-m*jnp.broadcast_to(r[t:t+1,:],(nb,n))
            y=y-m*jnp.broadcast_to(y[t:t+1,:],(nb,n))
        scale=lax.rsqrt(piv)
        u=jnp.where(lane>=sub+c0,r*scale,0.0); y=y*scale
        u_ref[c0:c0+nb,:]=u; m_ref[c0:c0+nb,:]=y
        if c0+nb<n:
            upd=mul(u.T,jnp.concatenate([u,y],1))
            a=a-upd[:,:n]; inv=inv-upd[:,n:]

def child_kernel(pos_ref, q0_ref, q1_ref, q2a_ref, q2b_ref, q3_ref, yt_ref, col_ref, ring_ref, a_ref, y_ref, u_ref, m_ref, sem_ref):
    front=pos_ref[0]; xpos=pos_ref[2]; nblk,prow,_=q0_ref.shape; n=BLK*nblk; half=nblk//2
    for d,first,ref in ((0,0,q0_ref),(1,0,q1_ref),(2,0,q2a_ref),(2,nblk//2,q2b_ref),(3,0,q3_ref)):
        at=pl.multiple_of(((xpos+d)%4)*prow,8)
        for k in range(ref.shape[0]):
            ring_ref[first+k,pl.ds(at,prow),:]=ref[k]
    for k in range(nblk):
        for i in range(half+1):
            r=(k+i)%nblk
            if r>k:
                if i<half: a_ref[k*BLK:(k+1)*BLK,r*BLK:(r+1)*BLK]=ring_ref[k,i*BLK:(i+1)*BLK,:].T
            else:
                a_ref[r*BLK:(r+1)*BLK,k*BLK:(k+1)*BLK]=ring_ref[k,i*BLK:(i+1)*BLK,:]
    y_ref[...]=jnp.zeros((n,n),jnp.float32)
    col_ref[...]=jnp.zeros((n,BLK),jnp.float32)
    def step(k,carry):
        for s in range(nblk):
            @pl.when(k==s)
            def _(s=s):
                m_ref[...]=a_ref[s*BLK:(s+1)*BLK,s*BLK:(s+1)*BLK]
        factor_block(m_ref[...],u_ref,m_ref,mm3)
        for s in range(nblk):
            @pl.when(k==s)
            def _(s=s):
                lo=s*BLK; hi=lo+BLK
                m=m_ref[...]
                parts=[]
                if s: parts.append(y_ref[lo:hi,:lo])
                if hi<n: parts.append(a_ref[lo:hi,hi:])
                full=mm3(m,jnp.concatenate(parts,1))
                yk=jnp.concatenate([full[:,:lo],m],1) if s else m
                y_ref[lo:hi,:hi]=yk
                pltpu.make_async_copy(y_ref.at[lo:hi],yt_ref.at[lo:hi],sem_ref.at[s]).start()
                rest=full[:,lo:]
                if hi<n:
                    upd=mm3(rest.T,jnp.concatenate([yk,rest],1))
                    y_ref[hi:,:hi]-=upd[:,:hi]
                    a_ref[hi:,hi:]-=upd[:,hi:n]
                @pl.when(front==s)
                def _():
                    col_ref[lo:hi,:]=u_ref[...].T
                    for j in range(s+1,nblk):
                        col_ref[j*BLK:(j+1)*BLK,:]=rest[:,(j-s-1)*BLK:(j-s)*BLK].T
        return carry
    lax.fori_loop(0,nblk,step,0)
    for s in range(nblk):
        pltpu.make_async_copy(y_ref.at[s*BLK:(s+1)*BLK],yt_ref.at[s*BLK:(s+1)*BLK],sem_ref.at[s]).wait()

def child_factor(pos,parts):
    nblk,prow,_=parts[0].shape; n=nblk*BLK; quarters=len(parts)-1
    vm=pl.BlockSpec(memory_space=pltpu.VMEM)
    return pl.pallas_call(child_kernel,
        out_shape=(pltpu.HBM((n,n),jnp.float32),jax.ShapeDtypeStruct((n,BLK),jnp.float32)),
        in_specs=[pl.BlockSpec(memory_space=pltpu.SMEM)]+[vm]*len(parts),
        out_specs=(pl.BlockSpec(memory_space=pltpu.HBM),vm),
        scratch_shapes=[pltpu.VMEM((nblk,quarters*prow,BLK),jnp.float32),pltpu.VMEM((n,n),jnp.float32),pltpu.VMEM((n,n),jnp.float32),pltpu.VMEM((BLK,BLK),jnp.float32),pltpu.VMEM((BLK,BLK),jnp.float32),pltpu.SemaphoreType.DMA((nblk,))],
        compiler_params=pltpu.CompilerParams(vmem_limit_bytes=30<<20),
        name="child_factor")(pos,*parts)


UPD=2

def update_kernel(pos_ref, *refs):
    far=refs[:9]; outs=refs[9:13]; near=refs[13:22]; zh_ref,zl_ref,sem_ref=refs[22:]
    fetch=[pltpu.make_async_copy(a.at[:,:b.shape[1]] if len(b.shape)==3 else a,b,sem_ref.at[i]) for i,(a,b) in enumerate(zip(far,near))]
    for i in (7,8,0,1,2,3,4,5,6): fetch[i].start()
    g=near[:7]; y_ref=near[7]; f_ref=near[8]
    n=y_ref.shape[0]
    zpos=pos_ref[1]; xpos=pos_ref[2]; planes=len(outs)
    dot=lambda x,y: jnp.dot(x,y,preferred_element_type=jnp.float32)
    fetch[7].wait()
    yh,yl=split(y_ref[...])
    fetch[8].wait()
    fh,fl=split(jnp.concatenate([f_ref[(xpos+d)%planes] for d in range(planes)],1))
    v=dot(yh,fh)+(dot(yh,fl)+dot(yl,fh))
    vh,vl=split(v.T)
    zt=dot(vh,yh)+(dot(vh,yl)+dot(vl,yh))
    zh,zl=split(zt)
    zh_ref[...]=zh; zl_ref[...]=zl
    zh,zl=split(y_ref[pl.ds(pl.multiple_of(zpos*BLK,BLK),BLK),:])
    for d in range(planes):
        @pl.when((xpos+d)%planes==0)
        def _(d=d):
            zh_ref[d*BLK:(d+1)*BLK]=zh; zl_ref[d*BLK:(d+1)*BLK]=zl
    for i in range(7): fetch[i].wait()
    blocks=[r[:n,:] for r in g]
    blocks.insert(4,jnp.concatenate([g[4][n:,:],g[3][n:,:]],0))
    for d in range(0,len(blocks),2):
        gh,gl=split(jnp.concatenate(blocks[d:d+2],1))
        prod=dot(zh_ref[...],gh)+(dot(zh_ref[...],gl)+dot(zl_ref[...],gh))
        for x in range(planes):
            for b in range(2):
                outs[x][(d+b)*BLK:(d+b+1)*BLK,:]=prod[x*BLK:(x+1)*BLK,b*BLK:(b+1)*BLK].T

def child_update(pos,gathered,y,rhs):
    piv=y.shape[0]; planes=rhs.shape[0]
    vm=pl.BlockSpec(memory_space=pltpu.VMEM); hbm=pl.BlockSpec(memory_space=pltpu.HBM)
    return pl.pallas_call(update_kernel,
        out_shape=(jax.ShapeDtypeStruct((piv,BLK),jnp.float32),)*planes,
        in_specs=[pl.BlockSpec(memory_space=pltpu.SMEM)]+[hbm]*(len(gathered)+2),
        out_specs=(vm,)*planes,
        scratch_shapes=[pltpu.VMEM(g.shape,jnp.float32) for g in gathered]+[pltpu.VMEM(y.shape,jnp.float32),pltpu.VMEM((planes,piv,BLK),jnp.float32),
            pltpu.VMEM((planes*BLK,piv),jnp.bfloat16),pltpu.VMEM((planes*BLK,piv),jnp.bfloat16),pltpu.SemaphoreType.DMA((len(gathered)+2,))],
        compiler_params=pltpu.CompilerParams(vmem_limit_bytes=44<<20),
        name="child_update")(pos,*[pltpu.with_memory_space_constraint(v,pltpu.HBM) for v in (*gathered,y,rhs)])

def combine_kernel(pos_ref, r0_ref, r1_ref, r2a_ref, r2b_ref, r3_ref, own_ref, col_ref, out_ref, sent_ref):
    zpos=pos_ref[1]; xpos=pos_ref[2]
    head=col_ref.shape[0]; nblk=r0_ref.shape[0]//BLK
    out_ref[:head,:]=col_ref[...]
    for d,first,ref in ((0,0,r0_ref),(1,0,r1_ref),(2,0,r2a_ref),(2,nblk//2,r2b_ref),(3,0,r3_ref)):
        src=(xpos-d+4)%4
        @pl.when(src>0)
        def _(first=first,ref=ref,src=src):
            for j in range(ref.shape[0]//BLK):
                blk=(zpos+first+j)%nblk
                at=pl.multiple_of(src*head+blk*BLK,BLK)
                r=ref[j*BLK:(j+1)*BLK,:]
                val=jnp.where(xpos==0,r,own_ref[pl.ds(at,BLK),:]-r)
                out_ref[pl.ds(at,BLK),:]=val
                sent_ref[blk,src-1]=val

def combine(pos,parts,own,col):
    vm=pl.BlockSpec(memory_space=pltpu.VMEM); nblk=parts[0].shape[0]//BLK
    return pl.pallas_call(combine_kernel,
        out_shape=(jax.ShapeDtypeStruct(own.shape,jnp.float32),jax.ShapeDtypeStruct((nblk,len(parts)-2,BLK,BLK),jnp.float32)),
        in_specs=[pl.BlockSpec(memory_space=pltpu.SMEM)]+[vm]*(2+len(parts)),
        out_specs=(vm,vm),
        compiler_params=pltpu.CompilerParams(vmem_limit_bytes=14<<20),
        name="combine")(pos,*parts,own,col)

def parent_kernel(pos_ref, e_ref, wc_ref, par_ref, out_ref, u_ref, m_ref, wr_ref, p11_ref):
    front=pos_ref[0]; leaf=pos_ref[1]
    slots=wr_ref.shape[0]; cs=wc_ref.shape[0]; xs=slots//cs
    for x in range(xs):
        for z in range(e_ref.shape[1]):
            first=8*(x*e_ref.shape[1]+z)
            for t in range(slots):
                wr_ref[(t%cs)*xs+t//cs,first:first+8,:]=e_ref[x,z,t]
            for p in range(PARENT_PIVOTS):
                p11_ref[p,first:first+8,:]=e_ref[x,z,slots+p]
    a0=p11_ref[0]; a1=p11_ref[1]
    factor_block(a0[:BLK],u_ref,m_ref,mm)
    m0=m_ref[...]; u00=u_ref[...]
    u01=mm(m0,a1[:BLK])
    u_ref[...]=a1[BLK:]-mm(u01.T,u01)
    factor_block(u_ref[...],u_ref,m_ref,mm)
    m1=m_ref[...]; u11=u_ref[...]
    w=jnp.concatenate([wc_ref[c] for c in range(cs)]+[wr_ref[s] for s in range(slots)],1)
    v0=mm(m0,w[:BLK])
    v1=mm(m1,w[BLK:]-mm(u01.T,v0))
    v=jnp.concatenate([v0,v1],0)
    lrows=v[:,cs*BLK:].T
    prod=mm(lrows,v[:,:cs*BLK])
    for s in range(slots):
        for c in range(cs):
            at=pl.ds(s*BLK*cs+c,BLK,stride=cs)
            out_ref[at,:]=par_ref[at,:]-prod[s*BLK:(s+1)*BLK,c*BLK:(c+1)*BLK]
    for p in range(PARENT_PIVOTS):
        @pl.when(front==p)
        def _(p=p):
            for s in range(slots):
                out_ref[pl.ds(s*BLK*cs,BLK,stride=cs),:]=lrows[s*BLK:(s+1)*BLK,p*BLK:(p+1)*BLK]
    top0=pl.ds(0,BLK,stride=cs)
    zero=jnp.zeros((BLK,BLK),jnp.float32)
    @pl.when(leaf<PARENT_PIVOTS)
    def _():
        for c in range(1,cs):
            out_ref[pl.ds(c,BLK,stride=cs),:]=zero
        @pl.when(front>=PARENT_PIVOTS)
        def _():
            out_ref[top0,:]=zero
        @pl.when((front==0)&(leaf==0))
        def _():
            out_ref[top0,:]=u00.T
        @pl.when((front==1)&(leaf==1))
        def _():
            out_ref[top0,:]=u11.T
        @pl.when((front==1)&(leaf==0))
        def _():
            out_ref[top0,:]=zero

def parent_base(pos,everything,wc,par):
    vm=pl.BlockSpec(memory_space=pltpu.VMEM)
    cs,rows,_=wc.shape; slots=everything.shape[2]-PARENT_PIVOTS
    return pl.pallas_call(parent_kernel,
        out_shape=jax.ShapeDtypeStruct(par.shape,jnp.float32),
        in_specs=[pl.BlockSpec(memory_space=pltpu.SMEM)]+[vm]*3,
        out_specs=vm,
        scratch_shapes=[pltpu.VMEM((BLK,BLK),jnp.float32),pltpu.VMEM((BLK,BLK),jnp.float32),
            pltpu.VMEM((slots,rows,BLK),jnp.float32),pltpu.VMEM((PARENT_PIVOTS,rows,BLK),jnp.float32)],
        compiler_params=pltpu.CompilerParams(vmem_limit_bytes=20<<20),
        name="parent_base")(pos,everything,wc,par)

def extend_kernel(idx_ref, flag_ref, base_ref, recv_ref, out_ref):
    out_ref[...]=base_ref[...]
    groups,quota=recv_ref.shape[0],recv_ref.shape[1]
    cs=PARENT_CSLOTS
    @pl.when(flag_ref[0]>0)
    def _():
        for q in range(quota):
            for g in range(groups):
                start=idx_ref[q,g]
                at=pl.ds(start,BLK,stride=cs)
                out_ref[at,:]+=recv_ref[g,q]

def extend_add(idx,flag,base,recv):
    vm=pl.BlockSpec(memory_space=pltpu.VMEM); sm=pl.BlockSpec(memory_space=pltpu.SMEM)
    return pl.pallas_call(extend_kernel,
        out_shape=jax.ShapeDtypeStruct(base.shape,jnp.float32),
        in_specs=[sm,sm,vm,vm], out_specs=vm,
        input_output_aliases={2:0},
        compiler_params=pltpu.CompilerParams(vmem_limit_bytes=14<<20),
        name="extend_add")(idx,flag,base,recv)

def body(child_fronts, parent_front, child_map):
    XS,ZS=4,8
    leaf=lax.axis_index("leaf"); front=lax.axis_index("front")
    xpos=front//ZS; zpos=front%ZS
    own=child_fronts.reshape(child_fronts.shape[1],BLK)
    piv=CHILD_PIVOTS*BLK
    top=own[:piv]
    xg=[[x*ZS+z for x in range(XS)] for z in range(ZS)]
    zg=[[x*ZS+z for z in range(ZS)] for x in range(XS)]
    def spread(v,groups):
        copies=jnp.broadcast_to(v[None],(len(groups[0]),)+v.shape)
        return lax.all_to_all(copies,"front",split_axis=0,concat_axis=0,tiled=True,axis_index_groups=groups)
    leaves=lax.axis_size("leaf"); fronts=XS*ZS
    tie=lax.optimization_barrier
    def swap(v,axis,groups=None):
        return lax.all_to_all(v,axis,split_axis=0,concat_axis=0,tiled=True,axis_index_groups=groups)
    def copies(v,n):
        return jnp.broadcast_to(v[None],(n,)+v.shape)
    part=(CHILD_PIVOTS//2+1)*BLK
    piece=lax.dynamic_slice_in_dim(jnp.concatenate([top,top],0),zpos*BLK,part,0)
    def hop(d):
        return [(x*ZS+z,((x+d)%XS)*ZS+z) for x in range(XS) for z in range(ZS)]
    def rot(d):
        return [(x*ZS+z,x*ZS+(z+d)%ZS) for x in range(XS) for z in range(ZS)]
    def fperm(pairs,v):
        return lax.ppermute(v,"front",pairs)
    quarters=piece.reshape(XS,part//XS,BLK)
    piece=quarters[0]
    for d in range(1,XS):
        piece=jnp.where(xpos==d,fperm([(z,d*ZS+z) for z in range(ZS)],quarters[d]),piece)
    prow=parent_front.reshape(parent_front.shape[0],BLK*PARENT_CSLOTS,BLK)
    wc=swap(copies(prow[0],leaves),"leaf")[:PARENT_PIVOTS]
    piece,wc=tie((piece,wc))
    quarter=swap(copies(piece,ZS),"front",zg)
    wc=wc.reshape(PARENT_PIVOTS*BLK,PARENT_CSLOTS,BLK).transpose(1,0,2)
    quarter,top1,wc=tie((quarter,top,wc))
    q3=fperm(hop(1),quarter); q1=fperm(hop(-1),quarter)
    g7=fperm(rot(1),top1); g1=fperm(rot(-1),top1)
    got=swap(wc.reshape(PARENT_CSLOTS,fronts,8,BLK).transpose(1,0,2,3),"front")
    mine=lax.dynamic_index_in_dim(got.reshape(XS,ZS,PARENT_CSLOTS,8,BLK),leaf,axis=1,keepdims=False)
    mine=jnp.concatenate([mine.reshape(XS*PARENT_CSLOTS,8,BLK),got[:PARENT_PIVOTS,0]],0)
    q1,q3,g1,g7,top1,mine=tie((q1,q3,g1,g7,top1,mine))
    q2a=fperm(hop(1),q3[:ZS//2]); q2b=fperm(hop(-1),q1[ZS//2:])
    half=piv//2
    g6=fperm(rot(2),top1); g2=fperm(rot(-2),top1)
    every=swap(copies(mine,ZS),"front",zg)
    q2a,q2b,top2,every,g2,g6=tie((q2a,q2b,top1,every,g2,g6))
    g5=fperm(rot(3),jnp.concatenate([top2,g7[:half]],0)); g3=fperm(rot(-3),jnp.concatenate([top2,g1[half:]],0))
    rhs=spread(jnp.concatenate([top2,every.reshape(-1,BLK)],0),xg)
    pos=jnp.stack([front,zpos,xpos]).astype(jnp.int32)
    y,col=child_factor(pos,[quarter,q1,q2a,q2b,q3])
    y,g2,g3,g5,g6,rhs=tie((y,g2,g3,g5,g6,rhs))
    p0,p1,p2,p3=child_update(pos,[top1,g1,g2,g3,g5,g6,g7],y,rhs)
    ra=fperm(hop(1),p2[:half]); rb=fperm(hop(-1),p2[half:])
    r1=fperm(hop(1),p1); r3=fperm(hop(-1),p3)
    ra,rb=tie((ra,rb))
    ra=fperm(hop(1),ra); rb=fperm(hop(-1),rb)
    out,sent=combine(pos,[p0,r1,ra,rb,r3],own,col)
    quota=(own.shape[0]-piv)//BLK//leaves
    recv=lax.all_to_all(sent,"leaf",split_axis=0,concat_axis=0,tiled=True)
    everything=rhs[:,piv:].reshape(XS,ZS,-1,8,BLK)
    base=parent_base(jnp.stack([front,leaf]).astype(jnp.int32),everything,wc,prow.reshape(-1,BLK))
    rowsel=(jnp.arange(leaves)==leaf)
    rmap=jnp.sum(jnp.where(rowsel[None,None,:],child_map.reshape(leaves,quota,leaves),0),axis=2)
    vblk=front-CHILD_PIVOTS
    csel=(jnp.arange(child_map.shape[1])==vblk)
    cmap=jnp.sum(jnp.where(csel[None,:],child_map,0),axis=1)
    idx=((rmap//leaves)*(BLK*PARENT_CSLOTS)+(cmap//32)[:,None]).T.astype(jnp.int32)
    flag=(front>=CHILD_PIVOTS).astype(jnp.int32).reshape(1)
    parent=extend_add(idx,flag,base,recv)
    return out.reshape(child_fronts.shape),parent.reshape(parent_front.shape)


def solution(mesh):
    return jax.shard_map(
        body,
        mesh=mesh,
        in_specs=(
            P("leaf", None, None, "front", None),
            P(None, "leaf", None, None, "front", None),
            P(),
        ),
        out_specs=(
            P("leaf", None, None, "front", None),
            P(None, "leaf", None, None, "front", None),
        ),
        check_vma=False,
    )
```

```python
import jax, jax.numpy as jnp
from jax import lax
from jax.experimental import pallas as pl
from jax.experimental.pallas import tpu as pltpu
from jax.sharding import PartitionSpec as P

BLK=128
CHILD_PIVOTS=8
PARENT_PIVOTS=2
PARENT_CSLOTS=2
NB=32
HI=lax.Precision.HIGHEST

def mm(a,b):
    return jnp.dot(a,b,precision=HI,preferred_element_type=jnp.float32)

def split(a):
    hi=a.astype(jnp.bfloat16)
    return hi,(a-hi.astype(jnp.float32)).astype(jnp.bfloat16)

def mm3(a,b):
    ah,al=split(a); bh,bl=split(b)
    dot=lambda x,y: jnp.dot(x,y,preferred_element_type=jnp.float32)
    return dot(ah,bh)+(dot(ah,bl)+dot(al,bh))

def factor_block(a, u_ref, m_ref, mul, nb=None):
    nb = nb or NB
    n=BLK
    rows=lax.broadcasted_iota(jnp.int32,(n,n),0); cols=lax.broadcasted_iota(jnp.int32,(n,n),1)
    inv=jnp.where(rows==cols,1.0,0.0).astype(jnp.float32)
    sub=lax.broadcasted_iota(jnp.int32,(nb,n),0)
    lane=lax.broadcasted_iota(jnp.int32,(nb,n),1)
    for c0 in range(0,n,nb):
        r=a[c0:c0+nb,:]; y=inv[c0:c0+nb,:]
        bc=[jnp.broadcast_to(r[:,c0+t:c0+t+1],(nb,n)) for t in range(nb)]
        piv=jnp.ones((nb,n),jnp.float32)
        for t in range(nb):
            p=jnp.broadcast_to(bc[t][t:t+1,:],(nb,n))
            piv=jnp.where(sub==t,p,piv)
            if t==nb-1: break
            m=jnp.where(sub>t,bc[t]*(1.0/p),0.0)
            for q in range(t+1,nb):
                bc[q]=bc[q]-m*jnp.broadcast_to(bc[q][t:t+1,:],(nb,n))
            r=r-m*jnp.broadcast_to(r[t:t+1,:],(nb,n))
            y=y-m*jnp.broadcast_to(y[t:t+1,:],(nb,n))
        scale=lax.rsqrt(piv)
        u=jnp.where(lane>=sub+c0,r*scale,0.0); y=y*scale
        u_ref[c0:c0+nb,:]=u; m_ref[c0:c0+nb,:]=y
        if c0+nb<n:
            upd=mul(u.T,jnp.concatenate([u,y],1))
            a=a-upd[:,:n]; inv=inv-upd[:,n:]

def child_kernel(pos_ref, q0_ref, q1_ref, q2a_ref, q2b_ref, q3_ref, yt_ref, col_ref, ring_ref, a_ref, y_ref, u_ref, m_ref, sem_ref):
    front=pos_ref[0]; xpos=pos_ref[2]; nblk,prow,_=q0_ref.shape; n=BLK*nblk; half=nblk//2
    for d,first,ref in ((0,0,q0_ref),(1,0,q1_ref),(2,0,q2a_ref),(2,nblk//2,q2b_ref),(3,0,q3_ref)):
        at=pl.multiple_of(((xpos+d)%4)*prow,8)
        for k in range(ref.shape[0]):
            ring_ref[first+k,pl.ds(at,prow),:]=ref[k]
    for k in range(nblk):
        for i in range(half+1):
            r=(k+i)%nblk
            if r>k:
                if i<half: a_ref[k*BLK:(k+1)*BLK,r*BLK:(r+1)*BLK]=ring_ref[k,i*BLK:(i+1)*BLK,:].T
            else:
                a_ref[r*BLK:(r+1)*BLK,k*BLK:(k+1)*BLK]=ring_ref[k,i*BLK:(i+1)*BLK,:]
    y_ref[...]=jnp.zeros((n,n),jnp.float32)
    col_ref[...]=jnp.zeros((n,BLK),jnp.float32)
    def step(k,carry):
        for s in range(nblk):
            @pl.when(k==s)
            def _(s=s):
                m_ref[...]=a_ref[s*BLK:(s+1)*BLK,s*BLK:(s+1)*BLK]
        factor_block(m_ref[...],u_ref,m_ref,mm3)
        for s in range(nblk):
            @pl.when(k==s)
            def _(s=s):
                lo=s*BLK; hi=lo+BLK
                m=m_ref[...]
                parts=[]
                if s: parts.append(y_ref[lo:hi,:lo])
                if hi<n: parts.append(a_ref[lo:hi,hi:])
                full=mm3(m,jnp.concatenate(parts,1))
                yk=jnp.concatenate([full[:,:lo],m],1) if s else m
                y_ref[lo:hi,:hi]=yk
                pltpu.make_async_copy(y_ref.at[lo:hi],yt_ref.at[lo:hi],sem_ref.at[s]).start()
                rest=full[:,lo:]
                if hi<n:
                    upd=mm3(rest.T,jnp.concatenate([yk,rest],1))
                    y_ref[hi:,:hi]-=upd[:,:hi]
                    a_ref[hi:,hi:]-=upd[:,hi:n]
                @pl.when(front==s)
                def _():
                    col_ref[lo:hi,:]=u_ref[...].T
                    for j in range(s+1,nblk):
                        col_ref[j*BLK:(j+1)*BLK,:]=rest[:,(j-s-1)*BLK:(j-s)*BLK].T
        return carry
    lax.fori_loop(0,nblk,step,0)
    for s in range(nblk):
        pltpu.make_async_copy(y_ref.at[s*BLK:(s+1)*BLK],yt_ref.at[s*BLK:(s+1)*BLK],sem_ref.at[s]).wait()

def child_factor(pos,parts):
    nblk,prow,_=parts[0].shape; n=nblk*BLK; quarters=len(parts)-1
    vm=pl.BlockSpec(memory_space=pltpu.VMEM)
    return pl.pallas_call(child_kernel,
        out_shape=(pltpu.HBM((n,n),jnp.float32),jax.ShapeDtypeStruct((n,BLK),jnp.float32)),
        in_specs=[pl.BlockSpec(memory_space=pltpu.SMEM)]+[vm]*len(parts),
        out_specs=(pl.BlockSpec(memory_space=pltpu.HBM),vm),
        scratch_shapes=[pltpu.VMEM((nblk,quarters*prow,BLK),jnp.float32),pltpu.VMEM((n,n),jnp.float32),pltpu.VMEM((n,n),jnp.float32),pltpu.VMEM((BLK,BLK),jnp.float32),pltpu.VMEM((BLK,BLK),jnp.float32),pltpu.SemaphoreType.DMA((nblk,))],
        compiler_params=pltpu.CompilerParams(vmem_limit_bytes=30<<20),
        name="child_factor")(pos,*parts)


UPD=2

def update_kernel(pos_ref, *refs):
    far=refs[:9]; outs=refs[9:13]; near=refs[13:22]; zh_ref,zl_ref,sem_ref=refs[22:]
    fetch=[pltpu.make_async_copy(a.at[:,:b.shape[1]] if len(b.shape)==3 else a,b,sem_ref.at[i]) for i,(a,b) in enumerate(zip(far,near))]
    for i in (7,8,0,1,2,3,4,5,6): fetch[i].start()
    g=near[:7]; y_ref=near[7]; f_ref=near[8]
    n=y_ref.shape[0]
    zpos=pos_ref[1]; xpos=pos_ref[2]; planes=len(outs)
    dot=lambda x,y: jnp.dot(x,y,preferred_element_type=jnp.float32)
    fetch[7].wait()
    yh,yl=split(y_ref[...])
    fetch[8].wait()
    fh,fl=split(jnp.concatenate([f_ref[(xpos+d)%planes] for d in range(planes)],1))
    v=dot(yh,fh)+(dot(yh,fl)+dot(yl,fh))
    vh,vl=split(v.T)
    zt=dot(vh,yh)+(dot(vh,yl)+dot(vl,yh))
    zh,zl=split(zt)
    zh_ref[...]=zh; zl_ref[...]=zl
    zh,zl=split(y_ref[pl.ds(pl.multiple_of(zpos*BLK,BLK),BLK),:])
    for d in range(planes):
        @pl.when((xpos+d)%planes==0)
        def _(d=d):
            zh_ref[d*BLK:(d+1)*BLK]=zh; zl_ref[d*BLK:(d+1)*BLK]=zl
    for i in range(7): fetch[i].wait()
    blocks=[r[:n,:] for r in g]
    blocks.insert(4,jnp.concatenate([g[4][n:,:],g[3][n:,:]],0))
    for d in range(0,len(blocks),2):
        gh,gl=split(jnp.concatenate(blocks[d:d+2],1))
        prod=dot(zh_ref[...],gh)+(dot(zh_ref[...],gl)+dot(zl_ref[...],gh))
        for x in range(planes):
            for b in range(2):
                outs[x][(d+b)*BLK:(d+b+1)*BLK,:]=prod[x*BLK:(x+1)*BLK,b*BLK:(b+1)*BLK].T

def child_update(pos,gathered,y,rhs):
    piv=y.shape[0]; planes=rhs.shape[0]
    vm=pl.BlockSpec(memory_space=pltpu.VMEM); hbm=pl.BlockSpec(memory_space=pltpu.HBM)
    return pl.pallas_call(update_kernel,
        out_shape=(jax.ShapeDtypeStruct((piv,BLK),jnp.float32),)*planes,
        in_specs=[pl.BlockSpec(memory_space=pltpu.SMEM)]+[hbm]*(len(gathered)+2),
        out_specs=(vm,)*planes,
        scratch_shapes=[pltpu.VMEM(g.shape,jnp.float32) for g in gathered]+[pltpu.VMEM(y.shape,jnp.float32),pltpu.VMEM((planes,piv,BLK),jnp.float32),
            pltpu.VMEM((planes*BLK,piv),jnp.bfloat16),pltpu.VMEM((planes*BLK,piv),jnp.bfloat16),pltpu.SemaphoreType.DMA((len(gathered)+2,))],
        compiler_params=pltpu.CompilerParams(vmem_limit_bytes=44<<20),
        name="child_update")(pos,*[pltpu.with_memory_space_constraint(v,pltpu.HBM) for v in (*gathered,y,rhs)])

def combine_kernel(pos_ref, r0_ref, r1_ref, r2a_ref, r2b_ref, r3_ref, own_ref, col_ref, out_ref, sent_ref):
    zpos=pos_ref[1]; xpos=pos_ref[2]
    head=col_ref.shape[0]; nblk=r0_ref.shape[0]//BLK
    out_ref[:head,:]=col_ref[...]
    for d,first,ref in ((0,0,r0_ref),(1,0,r1_ref),(2,0,r2a_ref),(2,nblk//2,r2b_ref),(3,0,r3_ref)):
        src=(xpos-d+4)%4
        @pl.when(src>0)
        def _(first=first,ref=ref,src=src):
            for j in range(ref.shape[0]//BLK):
                blk=(zpos+first+j)%nblk
                at=pl.multiple_of(src*head+blk*BLK,BLK)
                r=ref[j*BLK:(j+1)*BLK,:]
                val=jnp.where(xpos==0,r,own_ref[pl.ds(at,BLK),:]-r)
                out_ref[pl.ds(at,BLK),:]=val
                sent_ref[blk,src-1]=val

def combine(pos,parts,own,col):
    vm=pl.BlockSpec(memory_space=pltpu.VMEM); nblk=parts[0].shape[0]//BLK
    return pl.pallas_call(combine_kernel,
        out_shape=(jax.ShapeDtypeStruct(own.shape,jnp.float32),jax.ShapeDtypeStruct((nblk,len(parts)-2,BLK,BLK),jnp.float32)),
        in_specs=[pl.BlockSpec(memory_space=pltpu.SMEM)]+[vm]*(2+len(parts)),
        out_specs=(vm,vm),
        compiler_params=pltpu.CompilerParams(vmem_limit_bytes=14<<20),
        name="combine")(pos,*parts,own,col)

def parent_kernel(pos_ref, e_ref, wc_ref, par_ref, out_ref, u_ref, m_ref, wr_ref, p11_ref):
    front=pos_ref[0]; leaf=pos_ref[1]
    slots=wr_ref.shape[0]; cs=wc_ref.shape[0]; xs=slots//cs
    for x in range(xs):
        for z in range(e_ref.shape[1]):
            first=8*(x*e_ref.shape[1]+z)
            for t in range(slots):
                wr_ref[(t%cs)*xs+t//cs,first:first+8,:]=e_ref[x,z,t]
            for p in range(PARENT_PIVOTS):
                p11_ref[p,first:first+8,:]=e_ref[x,z,slots+p]
    a0=p11_ref[0]; a1=p11_ref[1]
    factor_block(a0[:BLK],u_ref,m_ref,mm)
    m0=m_ref[...]; u00=u_ref[...]
    u01=mm(m0,a1[:BLK])
    u_ref[...]=a1[BLK:]-mm(u01.T,u01)
    factor_block(u_ref[...],u_ref,m_ref,mm)
    m1=m_ref[...]; u11=u_ref[...]
    w=jnp.concatenate([wc_ref[c] for c in range(cs)]+[wr_ref[s] for s in range(slots)],1)
    v0=mm(m0,w[:BLK])
    v1=mm(m1,w[BLK:]-mm(u01.T,v0))
    v=jnp.concatenate([v0,v1],0)
    lrows=v[:,cs*BLK:].T
    prod=mm(lrows,v[:,:cs*BLK])
    for s in range(slots):
        for c in range(cs):
            at=pl.ds(s*BLK*cs+c,BLK,stride=cs)
            out_ref[at,:]=par_ref[at,:]-prod[s*BLK:(s+1)*BLK,c*BLK:(c+1)*BLK]
    for p in range(PARENT_PIVOTS):
        @pl.when(front==p)
        def _(p=p):
            for s in range(slots):
                out_ref[pl.ds(s*BLK*cs,BLK,stride=cs),:]=lrows[s*BLK:(s+1)*BLK,p*BLK:(p+1)*BLK]
    top0=pl.ds(0,BLK,stride=cs)
    zero=jnp.zeros((BLK,BLK),jnp.float32)
    @pl.when(leaf<PARENT_PIVOTS)
    def _():
        for c in range(1,cs):
            out_ref[pl.ds(c,BLK,stride=cs),:]=zero
        @pl.when(front>=PARENT_PIVOTS)
        def _():
            out_ref[top0,:]=zero
        @pl.when((front==0)&(leaf==0))
        def _():
            out_ref[top0,:]=u00.T
        @pl.when((front==1)&(leaf==1))
        def _():
            out_ref[top0,:]=u11.T
        @pl.when((front==1)&(leaf==0))
        def _():
            out_ref[top0,:]=zero

def parent_base(pos,everything,wc,par):
    vm=pl.BlockSpec(memory_space=pltpu.VMEM)
    cs,rows,_=wc.shape; slots=everything.shape[2]-PARENT_PIVOTS
    return pl.pallas_call(parent_kernel,
        out_shape=jax.ShapeDtypeStruct(par.shape,jnp.float32),
        in_specs=[pl.BlockSpec(memory_space=pltpu.SMEM)]+[vm]*3,
        out_specs=vm,
        scratch_shapes=[pltpu.VMEM((BLK,BLK),jnp.float32),pltpu.VMEM((BLK,BLK),jnp.float32),
            pltpu.VMEM((slots,rows,BLK),jnp.float32),pltpu.VMEM((PARENT_PIVOTS,rows,BLK),jnp.float32)],
        compiler_params=pltpu.CompilerParams(vmem_limit_bytes=20<<20),
        name="parent_base")(pos,everything,wc,par)

def extend_kernel(idx_ref, flag_ref, base_ref, recv_ref, out_ref):
    out_ref[...]=base_ref[...]
    groups,quota=recv_ref.shape[0],recv_ref.shape[1]
    cs=PARENT_CSLOTS
    @pl.when(flag_ref[0]>0)
    def _():
        for q in range(quota):
            for g in range(groups):
                start=idx_ref[q,g]
                at=pl.ds(start,BLK,stride=cs)
                out_ref[at,:]+=recv_ref[g,q]

def extend_add(idx,flag,base,recv):
    vm=pl.BlockSpec(memory_space=pltpu.VMEM); sm=pl.BlockSpec(memory_space=pltpu.SMEM)
    return pl.pallas_call(extend_kernel,
        out_shape=jax.ShapeDtypeStruct(base.shape,jnp.float32),
        in_specs=[sm,sm,vm,vm], out_specs=vm,
        input_output_aliases={2:0},
        compiler_params=pltpu.CompilerParams(vmem_limit_bytes=14<<20),
        name="extend_add")(idx,flag,base,recv)

def body(child_fronts, parent_front, child_map):
    XS,ZS=4,8
    leaf=lax.axis_index("leaf"); front=lax.axis_index("front")
    xpos=front//ZS; zpos=front%ZS
    own=child_fronts.reshape(child_fronts.shape[1],BLK)
    piv=CHILD_PIVOTS*BLK
    top=own[:piv]
    xg=[[x*ZS+z for x in range(XS)] for z in range(ZS)]
    zg=[[x*ZS+z for z in range(ZS)] for x in range(XS)]
    def spread(v,groups):
        copies=jnp.broadcast_to(v[None],(len(groups[0]),)+v.shape)
        return lax.all_to_all(copies,"front",split_axis=0,concat_axis=0,tiled=True,axis_index_groups=groups)
    leaves=lax.axis_size("leaf"); fronts=XS*ZS
    tie=lax.optimization_barrier
    def swap(v,axis,groups=None):
        return lax.all_to_all(v,axis,split_axis=0,concat_axis=0,tiled=True,axis_index_groups=groups)
    def copies(v,n):
        return jnp.broadcast_to(v[None],(n,)+v.shape)
    part=(CHILD_PIVOTS//2+1)*BLK
    piece=lax.dynamic_slice_in_dim(jnp.concatenate([top,top],0),zpos*BLK,part,0)
    def hop(d):
        return [(x*ZS+z,((x+d)%XS)*ZS+z) for x in range(XS) for z in range(ZS)]
    def rot(d):
        return [(x*ZS+z,x*ZS+(z+d)%ZS) for x in range(XS) for z in range(ZS)]
    def fperm(pairs,v):
        return lax.ppermute(v,"front",pairs)
    quarters=piece.reshape(XS,part//XS,BLK)
    piece=quarters[0]
    for d in range(1,XS):
        piece=jnp.where(xpos==d,fperm([(z,d*ZS+z) for z in range(ZS)],quarters[d]),piece)
    prow=parent_front.reshape(parent_front.shape[0],BLK*PARENT_CSLOTS,BLK)
    wc=swap(copies(prow[0],leaves),"leaf")[:PARENT_PIVOTS]
    g7=fperm(rot(1),top); g1=fperm(rot(-1),top)
    piece,wc,g7,g1=tie((piece,wc,g7,g1))
    quarter=swap(copies(piece,ZS),"front",zg)
    wc=wc.reshape(PARENT_PIVOTS*BLK,PARENT_CSLOTS,BLK).transpose(1,0,2)
    quarter,top1,wc=tie((quarter,top,wc))
    q3=fperm(hop(1),quarter); q1=fperm(hop(-1),quarter)
    g6=fperm(rot(2),top1); g2=fperm(rot(-2),top1)
    got=swap(wc.reshape(PARENT_CSLOTS,fronts,8,BLK).transpose(1,0,2,3),"front")
    mine=lax.dynamic_index_in_dim(got.reshape(XS,ZS,PARENT_CSLOTS,8,BLK),leaf,axis=1,keepdims=False)
    mine=jnp.concatenate([mine.reshape(XS*PARENT_CSLOTS,8,BLK),got[:PARENT_PIVOTS,0]],0)
    q1,q3,g2,g6,top1,mine=tie((q1,q3,g2,g6,top1,mine))
    q2a=fperm(hop(1),q3[:ZS//2]); q2b=fperm(hop(-1),q1[ZS//2:])
    half=piv//2
    every=swap(copies(mine,ZS),"front",zg)
    q2a,q2b,top2,every=tie((q2a,q2b,top1,every))
    g5=fperm(rot(3),jnp.concatenate([top2,g7[:half]],0)); g3=fperm(rot(-3),jnp.concatenate([top2,g1[half:]],0))
    rhs=spread(jnp.concatenate([top2,every.reshape(-1,BLK)],0),xg)
    pos=jnp.stack([front,zpos,xpos]).astype(jnp.int32)
    y,col=child_factor(pos,[quarter,q1,q2a,q2b,q3])
    y,g3,g5,rhs=tie((y,g3,g5,rhs))
    p0,p1,p2,p3=child_update(pos,[top1,g1,g2,g3,g5,g6,g7],y,rhs)
    ra=fperm(hop(1),p2[:half]); rb=fperm(hop(-1),p2[half:])
    r1=fperm(hop(1),p1); r3=fperm(hop(-1),p3)
    ra,rb=tie((ra,rb))
    ra=fperm(hop(1),ra); rb=fperm(hop(-1),rb)
    out,sent=combine(pos,[p0,r1,ra,rb,r3],own,col)
    quota=(own.shape[0]-piv)//BLK//leaves
    recv=lax.all_to_all(sent,"leaf",split_axis=0,concat_axis=0,tiled=True)
    everything=rhs[:,piv:].reshape(XS,ZS,-1,8,BLK)
    base=parent_base(jnp.stack([front,leaf]).astype(jnp.int32),everything,wc,prow.reshape(-1,BLK))
    rowsel=(jnp.arange(leaves)==leaf)
    rmap=jnp.sum(jnp.where(rowsel[None,None,:],child_map.reshape(leaves,quota,leaves),0),axis=2)
    vblk=front-CHILD_PIVOTS
    csel=(jnp.arange(child_map.shape[1])==vblk)
    cmap=jnp.sum(jnp.where(csel[None,:],child_map,0),axis=1)
    idx=((rmap//leaves)*(BLK*PARENT_CSLOTS)+(cmap//32)[:,None]).T.astype(jnp.int32)
    flag=(front>=CHILD_PIVOTS).astype(jnp.int32).reshape(1)
    parent=extend_add(idx,flag,base,recv)
    return out.reshape(child_fronts.shape),parent.reshape(parent_front.shape)


def solution(mesh):
    return jax.shard_map(
        body,
        mesh=mesh,
        in_specs=(
            P("leaf", None, None, "front", None),
            P(None, "leaf", None, None, "front", None),
            P(),
        ),
        out_specs=(
            P("leaf", None, None, "front", None),
            P(None, "leaf", None, None, "front", None),
        ),
        check_vma=False,
    )
```
